32 devices in a mesh: ckpt: 4 (over x, core), tensor: 8 (over z, y).
Axes of the slice: x: 2, y: 2, z: 4, core: 2. Of those that a mesh axis runs over, the one named last changes fastest.
Arguments:
- delta: bfloat16 [4, 2, 2048, 16384], P('ckpt', None, None, 'tensor'), may hold values from -0.03125 to 0.03125
- drop_mask: int32 [4, 2, 16, 128], P('ckpt', None, None, 'tensor'), may hold values 0 or 1
- scale_num: int32 [4], P('ckpt'), may hold values from 4 to 39
- base: bfloat16 [2, 2048, 16384], P(None, 'ckpt', 'tensor'), may hold values from -0.046875 to 0.046875
- tokens: bfloat16 [256, 16384], P(('tensor', 'ckpt')), may hold values from -6 to 6
Outputs:
- hidden: bfloat16 [256, 2048], P('tensor', 'ckpt')
The draws below stay inside these ranges and needn't reach their ends.
Inputs may be any that keep to these rules, and one draw needn't show every extreme that they name: drop_mask holds only 0 and 1. A checkpoint's scale is scale_num / 16.
All inputs are finite; a program needn't handle non-finite values. No bound on the sum of `drop_mask` on one device may be relied on, other than what follows from the above.
Results may differ from the reference program's by a relative error of at most 0.015.
Values may be sent and summed in bfloat16 or wider, within the bound.
No kernel may reach another device: no remote copies, remote signals or barrier semaphores. Data moves between devices by JAX's collectives and lax.ppermute only.
A program may use at most 192 MiB of HBM per device.

```python
import jax
import jax.numpy as jnp
from jax import lax

D = 16384
SLAB = 2048
BLOCK = 128
DEN = 16
CKPT = 4
TOKENS = 256


def plant(values, key, least, top_value):
    dims = values.shape
    spot = [jax.random.randint(jax.random.fold_in(key, axis), (), 0, dims[axis]) for axis in range(len(dims))]
    values = values.at[tuple(spot)].set(least)
    longest = dims.index(max(dims))
    spot[longest] = (spot[longest] + 1) % dims[longest]
    return values.at[tuple(spot)].set(top_value)


def spiked(values, key, source, target, shards_of, factor):
    owner, partner = [(jnp.arange(values.shape[position]) // (values.shape[position] // shards_of)).reshape([-1 if axis == position else 1 for axis in range(values.ndim)]) for position in (source, target)]
    chosen = jax.random.permutation(key, shards_of)[partner]
    strong = (owner == chosen) | (owner == (partner + shards_of // 2) % shards_of)
    return jnp.where(strong, factor * values, values)


def levels(rng, shape, pieces, low, high):
    level, own = 1.0, jax.random.fold_in(rng, 6)
    for axis_at, blocks in pieces:
        steps = jnp.exp(jax.random.uniform(jax.random.fold_in(own, axis_at), (blocks,), jnp.float32, low / len(pieces), high / len(pieces)))
        level = level * jnp.repeat(steps, shape[axis_at] // blocks).reshape([-1 if axis == axis_at else 1 for axis in range(len(shape))])
    return level


def scatter_about(stream_key, dims, scale, most, pieces=(), kind=jnp.bfloat16):
    drawn = jax.random.normal(stream_key, dims, jnp.float32) * scale
    if len(pieces) > 0:
        drawn = levels(stream_key, dims, pieces, -0.22, 0.18) * drawn
    return jnp.clip(drawn, min=-most, max=most).astype(kind)


def heavy_noise(key, dims, deviation, limit, pieces, heavy, kind=jnp.bfloat16):
    drawn = deviation * jax.random.normal(key, dims, jnp.float32)
    if pieces:
        drawn = drawn * levels(key, dims, pieces, -0.22, 0.18)
    return jnp.clip(spiked(drawn, jax.random.fold_in(key, 3), *heavy), -limit, limit).astype(kind)


def setup_inputs(seed: int = 0) -> dict:
    splits = jax.random.split(jax.random.key(seed), 6)
    delta = heavy_noise(splits[0], (CKPT, 2, SLAB, D), (D * CKPT) ** -0.5, 0.03125, ((0, 4), (3, 8)), (0, 2, 4, 2.0))
    drop_mask = plant((jax.random.randint(splits[1], (CKPT, 2, SLAB // BLOCK, D // BLOCK), 0, 2) < 1).astype(jnp.int32), jax.random.fold_in(splits[1], 1), 0, 1)
    scale_num = plant(jax.random.randint(splits[2], (CKPT,), 4, 40), jax.random.fold_in(splits[2], 1), 4, 39).astype(jnp.int32)
    base = scatter_about(splits[3], (2, SLAB, D), D ** -0.5, 0.046875, ((1, 4), (2, 8)))
    tokens = scatter_about(splits[4], (TOKENS, D), 1.0, 6.0, ((0, 32),))
    return dict(delta=delta, drop_mask=drop_mask, scale_num=scale_num, base=base, tokens=tokens)


def reference(delta, drop_mask, scale_num, base, tokens):
    def add_one(total, items):
        piece, mask, numer = items
        factor = mask.astype(jnp.float32) * (numer.astype(jnp.float32) / DEN)
        expanded = jnp.repeat(jnp.repeat(factor, BLOCK, axis=1), BLOCK, axis=2)
        term = (piece.astype(jnp.float32) * expanded).astype(jnp.bfloat16)
        return total + term.astype(jnp.float32), None

    start = jnp.zeros((2, SLAB, D), jnp.float32)
    total, unused = lax.scan(add_one, start, (delta, drop_mask, scale_num))
    merged = (base.astype(jnp.float32) + total).astype(jnp.bfloat16)
    gate = jnp.dot(tokens, merged[0].T, preferred_element_type=jnp.float32)
    up_proj = jnp.dot(tokens, merged[1].T, preferred_element_type=jnp.float32)
    return (jax.nn.silu(gate) * up_proj).astype(jnp.bfloat16)
```

```python
import functools

import jax
import jax.numpy as jnp
from jax import lax
from jax.experimental import pallas as pl
from jax.experimental.pallas import tpu as pltpu
from jax.sharding import PartitionSpec as P

BLOCK = 128
DEN = 16
CORES = 2
MIB = 1 << 20


def masked_rows(mask_ref, delta_ref, kept, m, row_block):
    for i in range(kept.shape[0] // BLOCK):
        for j in range(kept.shape[1] // BLOCK):
            keep = mask_ref[m, row_block * (kept.shape[0] // BLOCK) + i, j] != 0
            here = (slice(i * BLOCK, (i + 1) * BLOCK), slice(j * BLOCK, (j + 1) * BLOCK))
            piece = delta_ref[0, here[0], here[1]]
            kept[here] = jnp.where(keep, piece, jnp.zeros_like(piece))


def dot_rows(tokens, weights):
    return lax.dot_general(
        tokens, weights, (((1,), (1,)), ((), ())), preferred_element_type=jnp.float32
    )


def partial_kernel(with_base, rows, place_ref, scale_ref, mask_ref, own_ref, sib_ref, delta_ref, *rest):
    if with_base:
        base_ref, out_ref, held, kept = rest
    else:
        out_ref, held, kept = rest
    row, core = place_ref[0], place_ref[1]
    target = place_ref[2]
    step, m = pl.program_id(0), pl.program_id(1)

    @pl.when((step == 0) & (m == 0))
    def _():
        half = own_ref.shape[0]
        held[:half] = own_ref[...]
        held[half:] = sib_ref[...]

    masked_rows(mask_ref, delta_ref, kept, m, step * CORES + target)
    scale = scale_ref[0].astype(jnp.float32) / DEN

    def put(total):
        groups = out_ref.shape[1]
        split = total.reshape(CORES, -1, groups, rows, total.shape[-1])
        span = split.shape[1] * rows
        for side, at in ((0, core), (1, 1 - core)):
            for g in range(groups):
                piece = split[side, :, g].reshape(span, -1).astype(out_ref.dtype)
                out_ref[0, g, pl.ds(pl.multiple_of(at * span, span), span), :] = piece

    product = scale * dot_rows(held[...], kept[...])
    if with_base:

        @pl.when(step == row)
        def _():
            put(product + dot_rows(held[...], base_ref[0]))

        @pl.when(step != row)
        def _():
            put(product)

    else:
        put(product)


def partials(place, scale_num, mask, own, sib, delta, base, slab_own, groups, rows):
    width = delta.shape[2]
    owners = delta.shape[1] // slab_own // CORES
    span = 2 * own.shape[0] // groups
    whole = lambda *_: (0, 0)
    in_specs = [
        pl.BlockSpec(own.shape, whole),
        pl.BlockSpec(sib.shape, whole),
        pl.BlockSpec((1, slab_own, width), lambda x, m, place, *_: (m, x * CORES + place[2], 0)),
    ]
    operands = [own, sib, delta]
    if base is not None:
        in_specs.append(pl.BlockSpec((1, slab_own, width), lambda x, m, *_: (m, 0, 0)))
        operands.append(base)
    out_dtype = jnp.bfloat16 if base is None else jnp.float32
    flops = 2 * 2 * own.shape[0] * width * 2 * slab_own * owners
    return pl.pallas_call(
        functools.partial(partial_kernel, base is not None, rows),
        out_shape=jax.ShapeDtypeStruct((owners, groups, span, 2 * slab_own), out_dtype),
        grid_spec=pltpu.PrefetchScalarGridSpec(
            num_scalar_prefetch=3,
            grid=(owners, 2),
            in_specs=in_specs,
            out_specs=pl.BlockSpec((1, groups, span, slab_own), lambda x, m, *_: (x, 0, 0, m)),
            scratch_shapes=[
                pltpu.VMEM((2 * own.shape[0], width), jnp.bfloat16),
                pltpu.VMEM((slab_own, width), jnp.bfloat16),
            ],
        ),
        compiler_params=pltpu.CompilerParams(vmem_limit_bytes=40 * MIB),
        cost_estimate=pl.CostEstimate(
            flops=flops, bytes_accessed=2 * slab_own * owners * width * 2, transcendentals=0
        ),
    )(place, scale_num, mask, *operands)


def finish_kernel(rows, part_ref, out_ref, total):
    step = pl.program_id(0)
    here = jnp.sum(part_ref[...].astype(jnp.float32), axis=0)

    @pl.when(step == 0)
    def _():
        total[...] = here

    @pl.when(step != 0)
    def _():
        total[...] += here

    @pl.when(step == pl.num_programs(0) - 1)
    def _():
        slab_own = out_ref.shape[1]
        gate, up = total[:, :slab_own], total[:, slab_own:]
        value = gate / (1 + jnp.exp(-gate)) * up
        split = value.reshape(CORES, -1, rows, slab_own)
        pieces = [split[core, x] for x in range(split.shape[1]) for core in range(CORES)]
        out_ref[...] = jnp.concatenate(pieces, axis=0).astype(out_ref.dtype)


def finish(parts, rows):
    sources, span, both = parts.shape
    block = min(sources, 16)
    return pl.pallas_call(
        functools.partial(finish_kernel, rows),
        out_shape=jax.ShapeDtypeStruct((span, both // 2), jnp.bfloat16),
        grid=(sources // block,),
        in_specs=[pl.BlockSpec((block, span, both), lambda i: (i, 0, 0))],
        out_specs=pl.BlockSpec((span, both // 2), lambda i: (0, 0)),
        scratch_shapes=[pltpu.VMEM((span, both), jnp.float32)],
        compiler_params=pltpu.CompilerParams(vmem_limit_bytes=32 * MIB),
        cost_estimate=pl.CostEstimate(
            flops=parts.size, bytes_accessed=2 * parts.size, transcendentals=span * both // 2
        ),
    )(parts)


def solution(mesh):
    ckpts, groups = mesh.shape["ckpt"], mesh.shape["tensor"]
    owners = ckpts // CORES
    both = ("ckpt", "tensor")
    same_core = [
        [(x * CORES + core) * groups + t for x in range(owners) for t in range(groups)]
        for core in range(CORES)
    ]
    swap = [(i, i ^ 1) for i in range(ckpts)]

    def local(delta, drop_mask, scale_num, base, tokens):
        rows, width = tokens.shape
        width //= groups
        slab_own = base.shape[1]
        me = lax.axis_index("ckpt")
        row, core = me // CORES, me % CORES

        cut = tokens.reshape(rows, groups, width).transpose(1, 0, 2)
        send = jnp.broadcast_to(cut[None], (owners, groups, rows, width)).reshape(-1, rows, width)
        own = lax.all_to_all(send, both, 0, 0, axis_index_groups=same_core, tiled=True)
        own = own.reshape(owners * groups * rows, width)
        sib = lax.ppermute(own, "ckpt", swap)

        place = jnp.stack([row, core, 1 - core]).astype(jnp.int32)
        theirs = partials(
            place, scale_num, drop_mask[0], own, sib, delta[0], None, slab_own, groups, rows
        )
        arrived = lax.ppermute(theirs, "ckpt", swap)
        place = jnp.stack([row, core, core]).astype(jnp.int32)
        ours = partials(
            place, scale_num, drop_mask[0], own, sib, delta[0], base, slab_own, groups, rows
        )
        chip = (ours + arrived.astype(jnp.float32)).astype(jnp.bfloat16)
        chip = chip.reshape(owners * groups, -1, 2 * slab_own)
        parts = lax.all_to_all(chip, both, 0, 0, axis_index_groups=same_core, tiled=True)
        return finish(parts, rows)

    in_specs = (
        P("ckpt", None, None, "tensor"),
        P("ckpt", None, None, "tensor"),
        P("ckpt"),
        P(None, "ckpt", "tensor"),
        P(("tensor", "ckpt"), None),
    )
    out_specs = P("tensor", "ckpt")
    return jax.shard_map(local, mesh=mesh, in_specs=in_specs, out_specs=out_specs, check_vma=False)
```

```python
import functools

import jax
import jax.numpy as jnp
from jax import lax
from jax.experimental import pallas as pl
from jax.experimental.pallas import tpu as pltpu
from jax.sharding import PartitionSpec as P

BLOCK = 128
DEN = 16
CORES = 2
MIB = 1 << 20
VMEM = pl.BlockSpec(memory_space=pltpu.VMEM)
SMEM = pl.BlockSpec(memory_space=pltpu.SMEM)
HBM = pl.BlockSpec(memory_space=pltpu.HBM)


def dot_rows(tokens, weights):
    return lax.dot_general(
        tokens, weights, (((1,), (1,)), ((), ())), preferred_element_type=jnp.float32
    )


def silu_times(gate, up):
    return gate / (1 + jnp.exp(-gate)) * up


def gather_held(held, pieces):
    for i, piece in enumerate(pieces):
        span = piece.shape[0]
        held[i * span : (i + 1) * span] = piece[...]


def drop_blocks(mask_ref, kept, part, m, first):
    rows, width = kept.shape[1:]
    for i in range(rows // BLOCK):
        for j in range(width // BLOCK):
            here = (part, slice(i * BLOCK, (i + 1) * BLOCK), slice(j * BLOCK, (j + 1) * BLOCK))
            piece = kept[here]
            keep = mask_ref[m, first * (rows // BLOCK) + i, j] != 0
            kept[here] = jnp.where(keep, piece, jnp.zeros_like(piece))


def put(view, total, core):
    groups, rows = view.shape[-5 if len(view.shape) == 5 else 0], view.shape[-2]
    split = total.reshape(-1, CORES, groups, rows, total.shape[-1])
    for x in range(split.shape[0]):
        for side in range(CORES):
            at = core if side == 0 else 1 - core
            for g in range(groups):
                here = (g, at) if len(view.shape) == 4 else (g, x, at)
                view[here] = split[x, side, g].astype(view.dtype)


def half_of(ref, m):
    size = ref.shape[-1] // 2
    return ref.at[(slice(None),) * (len(ref.shape) - 1) + (slice(m * size, (m + 1) * size),)]


def fetch(delta, kept, sems, owners, chunks):
    slab_own = kept.shape[1]
    span = slab_own // chunks
    copies = []
    for part, (m, owner) in enumerate(owners):
        for h in range(chunks):
            rows = pl.ds(pl.multiple_of(owner * slab_own + h * span, span), span)
            copy = pltpu.make_async_copy(
                delta.at[m, rows, :], kept.at[part, pl.ds(h * span, span), :], sems.at[part, h]
            )
            copy.start()
            copies.append(copy)
    return copies


def owners_of(chip, core):
    return [(m, chip * CORES + core) for m in range(2)]


def wait_for(copies, part, chunks):
    for copy in copies[part * chunks : (part + 1) * chunks]:
        copy.wait()


def early_kernel(
    place, scale_num, mask_hbm, own, sib, delta, theirs, ours, kept, held, mask, sems, mask_sem
):
    chip, core = place[0], place[1]
    chunks = sems.shape[1]
    mask_copy = pltpu.make_async_copy(mask_hbm, mask, mask_sem)
    mask_copy.start()
    owners = owners_of(1 - chip, 1 - core) + owners_of(1 - chip, core)
    copies = fetch(delta, kept, sems, owners, chunks)
    gather_held(held, (own, sib))
    scale = scale_num[0].astype(jnp.float32) / DEN
    mask_copy.wait()
    for part, (m, owner) in enumerate(owners):
        wait_for(copies, part, chunks)
        drop_blocks(mask, kept, part, m, owner)
        total = scale * dot_rows(held[...], kept[part])
        put(half_of(theirs if part < 2 else ours, m), total, core)


def later_kernel(
    place, scale_num, mask_hbm, own, sib, far_own, far_sib, kept, delta, theirs, ours, theirs_home,
    home, held, mask, sems, mask_sem,
):
    chip, core = place[0], place[1]
    chunks = sems.shape[1]
    half = held.shape[0] // 2
    mask_copy = pltpu.make_async_copy(mask_hbm, mask, mask_sem)
    mask_copy.start()
    owners = owners_of(chip, 1 - core)
    copies = fetch(delta, home, sems, owners, chunks)
    gather_held(held, (own, sib, far_own, far_sib))
    scale = scale_num[0].astype(jnp.float32) / DEN
    for part in range(4):
        total = scale * dot_rows(held[half:], kept[part])
        put(half_of(theirs if part < 2 else ours, part % 2), total, core)
    mask_copy.wait()
    for part, (m, owner) in enumerate(owners):
        wait_for(copies, part, chunks)
        drop_blocks(mask, home, part, m, owner)
        put(half_of(theirs_home, m), scale * dot_rows(held[...], home[part]), core)


def home_kernel(
    place, scale_num, mask_hbm, own, sib, far_own, far_sib, delta, base, ours,
    kept, kept_base, held, mask, sems, base_sems, mask_sem,
):
    chip, core = place[0], place[1]
    chunks = sems.shape[1]
    mask_copy = pltpu.make_async_copy(mask_hbm, mask, mask_sem)
    mask_copy.start()
    owners = owners_of(chip, core)
    copies = fetch(delta, kept, sems, owners, chunks)
    base_copies = fetch(base, kept_base, base_sems, [(0, 0), (1, 0)], chunks)
    gather_held(held, (own, sib, far_own, far_sib))
    scale = scale_num[0].astype(jnp.float32) / DEN
    mask_copy.wait()
    for part, (m, owner) in enumerate(owners):
        wait_for(copies, part, chunks)
        drop_blocks(mask, kept, part, m, owner)
        total = scale * dot_rows(held[...], kept[part])
        wait_for(base_copies, part, chunks)
        put(half_of(ours, m), total + dot_rows(held[...], kept_base[m]), core)


def call(kernel, outs, scratch, in_specs, operands, flops, traffic):
    return pl.pallas_call(
        kernel,
        out_shape=outs,
        in_specs=in_specs,
        out_specs=[VMEM] * len(outs),
        scratch_shapes=scratch,
        compiler_params=pltpu.CompilerParams(vmem_limit_bytes=50 * MIB),
        cost_estimate=pl.CostEstimate(flops=flops // 8, bytes_accessed=traffic // 8, transcendentals=0),
    )(*operands)


def join_kernel(ours, arrived, out):
    out[...] = (ours[...] + arrived[...].astype(jnp.float32)).astype(out.dtype)


def join_home_kernel(ours, arrived, near, far, out):
    for x, other in enumerate((near, far)):
        total = ours[:, x] + arrived[:, x].astype(jnp.float32) + other[...].astype(jnp.float32)
        out[:, x] = total.astype(out.dtype)


def last_kernel(place, parts, out, total):
    chip, core = place[0], place[1]
    rows = parts.shape[-2]
    slab_own = out.shape[1]
    for x in range(2):
        at = chip if x == 0 else 1 - chip
        for c in range(CORES):
            both = jnp.sum(parts[:, x, c].astype(jnp.float32), axis=0)
            value = silu_times(both[:, :slab_own], both[:, slab_own:])
            total[pl.ds(pl.multiple_of((at * CORES + c) * rows, rows), rows), :] = value
    out[...] = total[...].astype(out.dtype)


def local_pair(delta, drop_mask, scale_num, base, tokens, *, groups):
    rows, width = tokens.shape[0], tokens.shape[1] // groups
    slab_own = base.shape[1]
    f32, bf16 = jnp.float32, jnp.bfloat16
    me = lax.axis_index("ckpt")
    place = jnp.stack([me >> 1, me & 1]).astype(jnp.int32)
    mask, delta = drop_mask[0], delta[0]
    core_swap = functools.partial(lax.ppermute, axis_name="ckpt", perm=[(i, i ^ 1) for i in range(4)])
    chip_swap = functools.partial(lax.ppermute, axis_name="ckpt", perm=[(i, i ^ 2) for i in range(4)])

    cut = tokens.reshape(rows, groups, width).transpose(1, 0, 2)
    own = lax.all_to_all(cut, "tensor", 0, 0, tiled=True).reshape(groups * rows, width)
    far_own = chip_swap(own)
    sib = core_swap(own)

    half = groups * rows * CORES
    chunks = 2
    part = jax.ShapeDtypeStruct
    pair = (groups, CORES, rows, 2 * slab_own)
    four = (groups, 2, CORES, rows, 2 * slab_own)
    weights = (4, slab_own, width)
    size = 4 * slab_own * width
    theirs, ours, kept = call(
        early_kernel,
        [part(pair, bf16), part(pair, f32), part(weights, bf16)],
        [
            pltpu.VMEM((half, width), bf16),
            pltpu.SMEM(mask.shape, mask.dtype),
            pltpu.SemaphoreType.DMA((4, chunks)),
            pltpu.SemaphoreType.DMA(()),
        ],
        [SMEM, SMEM, HBM, VMEM, VMEM, HBM],
        (place, scale_num, mask, own, sib, delta),
        2 * half * size,
        2 * size,
    )
    near = core_swap(theirs)
    far_own, theirs = lax.optimization_barrier((far_own, theirs))
    far_sib = core_swap(far_own)
    simple = lambda kernel, shape, *xs: pl.pallas_call(
        kernel,
        out_shape=part(shape, bf16),
        in_specs=[VMEM] * len(xs),
        out_specs=VMEM,
        compiler_params=pltpu.CompilerParams(vmem_limit_bytes=16 * MIB),
        cost_estimate=pl.CostEstimate(flops=xs[0].size, bytes_accessed=8 * xs[0].size, transcendentals=0),
    )(*xs)
    first, far_sib = lax.optimization_barrier((simple(join_kernel, pair, ours, near), far_sib))
    over_first = chip_swap(first)
    theirs, ours, theirs_home = call(
        later_kernel,
        [part(pair, bf16), part(pair, f32), part(four, bf16)],
        [
            pltpu.VMEM((2, slab_own, width), bf16),
            pltpu.VMEM((2 * half, width), bf16),
            pltpu.SMEM(mask.shape, mask.dtype),
            pltpu.SemaphoreType.DMA((2, chunks)),
            pltpu.SemaphoreType.DMA(()),
        ],
        [SMEM, SMEM, HBM, VMEM, VMEM, VMEM, VMEM, VMEM, HBM],
        (place, scale_num, mask, own, sib, far_own, far_sib, kept, delta),
        4 * half * size,
        2 * size,
    )
    theirs, theirs_home, over_first = lax.optimization_barrier((theirs, theirs_home, over_first))
    second = simple(join_kernel, pair, ours, core_swap(theirs))
    near_home = core_swap(theirs_home)
    second, own = lax.optimization_barrier((second, own))
    over_second = chip_swap(second)
    (ours,) = call(
        home_kernel,
        [part(four, f32)],
        [
            pltpu.VMEM((2, slab_own, width), bf16),
            pltpu.VMEM((2, slab_own, width), bf16),
            pltpu.VMEM((2 * half, width), bf16),
            pltpu.SMEM(mask.shape, mask.dtype),
            pltpu.SemaphoreType.DMA((2, chunks)),
            pltpu.SemaphoreType.DMA((2, chunks)),
            pltpu.SemaphoreType.DMA(()),
        ],
        [SMEM, SMEM, HBM, VMEM, VMEM, VMEM, VMEM, HBM, HBM],
        (place, scale_num, mask, own, sib, far_own, far_sib, delta, base),
        4 * half * size,
        2 * size,
    )
    whole = simple(join_home_kernel, four, ours, near_home, over_second, over_first)
    parts = lax.all_to_all(whole, "tensor", 0, 0, tiled=True)
    return pl.pallas_call(
        last_kernel,
        out_shape=part((2 * CORES * rows, slab_own), bf16),
        in_specs=[SMEM, VMEM],
        out_specs=VMEM,
        scratch_shapes=[pltpu.VMEM((2 * CORES * rows, slab_own), f32)],
        compiler_params=pltpu.CompilerParams(vmem_limit_bytes=16 * MIB),
    )(place, parts)


def masked_rows(mask_ref, delta_ref, kept, m, row_block):
    for i in range(kept.shape[0] // BLOCK):
        for j in range(kept.shape[1] // BLOCK):
            keep = mask_ref[m, row_block * (kept.shape[0] // BLOCK) + i, j] != 0
            here = (slice(i * BLOCK, (i + 1) * BLOCK), slice(j * BLOCK, (j + 1) * BLOCK))
            piece = delta_ref[0, here[0], here[1]]
            kept[here] = jnp.where(keep, piece, jnp.zeros_like(piece))


def partial_kernel(with_base, rows, place_ref, scale_ref, mask_ref, own_ref, sib_ref, delta_ref, *rest):
    if with_base:
        base_ref, out_ref, held, kept = rest
    else:
        out_ref, held, kept = rest
    row, core = place_ref[0], place_ref[1]
    target = place_ref[2]
    step, m = pl.program_id(0), pl.program_id(1)

    @pl.when((step == 0) & (m == 0))
    def _():
        half = own_ref.shape[0]
        held[:half] = own_ref[...]
        held[half:] = sib_ref[...]

    masked_rows(mask_ref, delta_ref, kept, m, step * CORES + target)
    scale = scale_ref[0].astype(jnp.float32) / DEN

    def store(total):
        groups = out_ref.shape[1]
        split = total.reshape(CORES, -1, groups, rows, total.shape[-1])
        span = split.shape[1] * rows
        for side, at in ((0, core), (1, 1 - core)):
            for g in range(groups):
                piece = split[side, :, g].reshape(span, -1).astype(out_ref.dtype)
                out_ref[0, g, pl.ds(pl.multiple_of(at * span, span), span), :] = piece

    product = scale * dot_rows(held[...], kept[...])
    if with_base:

        @pl.when(step == row)
        def _():
            store(product + dot_rows(held[...], base_ref[0]))

        @pl.when(step != row)
        def _():
            store(product)

    else:
        store(product)


def partials(place, scale_num, mask, own, sib, delta, base, slab_own, groups, rows):
    width = delta.shape[2]
    owners = delta.shape[1] // slab_own // CORES
    span = 2 * own.shape[0] // groups
    whole = lambda *_: (0, 0)
    in_specs = [
        pl.BlockSpec(own.shape, whole),
        pl.BlockSpec(sib.shape, whole),
        pl.BlockSpec((1, slab_own, width), lambda x, m, place, *_: (m, x * CORES + place[2], 0)),
    ]
    operands = [own, sib, delta]
    if base is not None:
        in_specs.append(pl.BlockSpec((1, slab_own, width), lambda x, m, *_: (m, 0, 0)))
        operands.append(base)
    out_dtype = jnp.bfloat16 if base is None else jnp.float32
    flops = 2 * 2 * own.shape[0] * width * 2 * slab_own * owners
    return pl.pallas_call(
        functools.partial(partial_kernel, base is not None, rows),
        out_shape=jax.ShapeDtypeStruct((owners, groups, span, 2 * slab_own), out_dtype),
        grid_spec=pltpu.PrefetchScalarGridSpec(
            num_scalar_prefetch=3,
            grid=(owners, 2),
            in_specs=in_specs,
            out_specs=pl.BlockSpec((1, groups, span, slab_own), lambda x, m, *_: (x, 0, 0, m)),
            scratch_shapes=[
                pltpu.VMEM((2 * own.shape[0], width), jnp.bfloat16),
                pltpu.VMEM((slab_own, width), jnp.bfloat16),
            ],
        ),
        compiler_params=pltpu.CompilerParams(vmem_limit_bytes=40 * MIB),
        cost_estimate=pl.CostEstimate(
            flops=flops, bytes_accessed=2 * slab_own * owners * width * 2, transcendentals=0
        ),
    )(place, scale_num, mask, *operands)


def finish_kernel(rows, part_ref, out_ref, total):
    step = pl.program_id(0)
    here = jnp.sum(part_ref[...].astype(jnp.float32), axis=0)

    @pl.when(step == 0)
    def _():
        total[...] = here

    @pl.when(step != 0)
    def _():
        total[...] += here

    @pl.when(step == pl.num_programs(0) - 1)
    def _():
        slab_own = out_ref.shape[1]
        value = silu_times(total[:, :slab_own], total[:, slab_own:])
        split = value.reshape(CORES, -1, rows, slab_own)
        pieces = [split[core, x] for x in range(split.shape[1]) for core in range(CORES)]
        out_ref[...] = jnp.concatenate(pieces, axis=0).astype(out_ref.dtype)


def finish(parts, rows):
    sources, span, both = parts.shape
    block = min(sources, 16)
    return pl.pallas_call(
        functools.partial(finish_kernel, rows),
        out_shape=jax.ShapeDtypeStruct((span, both // 2), jnp.bfloat16),
        grid=(sources // block,),
        in_specs=[pl.BlockSpec((block, span, both), lambda i: (i, 0, 0))],
        out_specs=pl.BlockSpec((span, both // 2), lambda i: (0, 0)),
        scratch_shapes=[pltpu.VMEM((span, both), jnp.float32)],
        compiler_params=pltpu.CompilerParams(vmem_limit_bytes=32 * MIB),
        cost_estimate=pl.CostEstimate(
            flops=parts.size, bytes_accessed=2 * parts.size, transcendentals=span * both // 2
        ),
    )(parts)


def local_any(delta, drop_mask, scale_num, base, tokens, *, ckpts, groups):
    owners = ckpts // CORES
    both = ("ckpt", "tensor")
    same_core = [
        [(x * CORES + core) * groups + t for x in range(owners) for t in range(groups)]
        for core in range(CORES)
    ]
    swap = [(i, i ^ 1) for i in range(ckpts)]
    rows, width = tokens.shape
    width //= groups
    slab_own = base.shape[1]
    me = lax.axis_index("ckpt")
    row, core = me // CORES, me % CORES

    cut = tokens.reshape(rows, groups, width).transpose(1, 0, 2)
    send = jnp.broadcast_to(cut[None], (owners, groups, rows, width)).reshape(-1, rows, width)
    own = lax.all_to_all(send, both, 0, 0, axis_index_groups=same_core, tiled=True)
    own = own.reshape(owners * groups * rows, width)
    sib = lax.ppermute(own, "ckpt", swap)

    common = (own, sib, delta[0])
    place = jnp.stack([row, core, 1 - core]).astype(jnp.int32)
    theirs = partials(place, scale_num, drop_mask[0], *common, None, slab_own, groups, rows)
    arrived = lax.ppermute(theirs, "ckpt", swap)
    place = jnp.stack([row, core, core]).astype(jnp.int32)
    ours = partials(place, scale_num, drop_mask[0], *common, base, slab_own, groups, rows)
    chip = (ours + arrived.astype(jnp.float32)).astype(jnp.bfloat16)
    chip = chip.reshape(owners * groups, -1, 2 * slab_own)
    parts = lax.all_to_all(chip, both, 0, 0, axis_index_groups=same_core, tiled=True)
    return finish(parts, rows)


def solution(mesh):
    ckpts, groups = mesh.shape["ckpt"], mesh.shape["tensor"]
    if ckpts == 2 * CORES:
        local = functools.partial(local_pair, groups=groups)
    else:
        local = functools.partial(local_any, ckpts=ckpts, groups=groups)
    in_specs = (
        P("ckpt", None, None, "tensor"),
        P("ckpt", None, None, "tensor"),
        P("ckpt"),
        P(None, "ckpt", "tensor"),
        P(("tensor", "ckpt"), None),
    )
    out_specs = P("tensor", "ckpt")
    return jax.shard_map(local, mesh=mesh, in_specs=in_specs, out_specs=out_specs, check_vma=False)
```

```python
import functools

import jax
import jax.numpy as jnp
from jax import lax
from jax.experimental import pallas as pl
from jax.experimental.pallas import tpu as pltpu
from jax.sharding import PartitionSpec as P

BLOCK = 128
DEN = 16
CORES = 2
MIB = 1 << 20
VMEM = pl.BlockSpec(memory_space=pltpu.VMEM)
SMEM = pl.BlockSpec(memory_space=pltpu.SMEM)
HBM = pl.BlockSpec(memory_space=pltpu.HBM)


def dot_rows(tokens, weights):
    return lax.dot_general(
        tokens, weights, (((1,), (1,)), ((), ())), preferred_element_type=jnp.float32
    )


def silu_times(gate, up):
    return gate / (1 + jnp.exp(-gate)) * up


def gather_held(held, pieces):
    for i, piece in enumerate(pieces):
        span = piece.shape[0]
        held[i * span : (i + 1) * span] = piece[...]


def kept_blocks(mask_ref, weights, m, owner):
    rows, width = weights.shape
    strips = []
    for i in range(rows // BLOCK):
        strip = []
        for j in range(width // BLOCK):
            piece = weights[i * BLOCK : (i + 1) * BLOCK, j * BLOCK : (j + 1) * BLOCK]
            keep = mask_ref[m, owner * (rows // BLOCK) + i, j] != 0
            strip.append(jnp.where(keep, piece, jnp.zeros_like(piece)))
        strips.append(jnp.concatenate(strip, axis=1))
    return jnp.concatenate(strips, axis=0)


def put(view, total, core):
    groups, rows = view.shape[-5 if len(view.shape) == 5 else 0], view.shape[-2]
    split = total.reshape(-1, CORES, groups, rows, total.shape[-1])
    for x in range(split.shape[0]):
        for side in range(CORES):
            at = core if side == 0 else 1 - core
            for g in range(groups):
                here = (g, at) if len(view.shape) == 4 else (g, x, at)
                view[here] = split[x, side, g].astype(view.dtype)


def half_of(ref, m):
    size = ref.shape[-1] // 2
    return ref.at[(slice(None),) * (len(ref.shape) - 1) + (slice(m * size, (m + 1) * size),)]


def fetch(delta, kept, sems, owners, chunks):
    slab_own = kept.shape[1]
    span = slab_own // chunks
    copies = []
    for part, (m, owner) in enumerate(owners):
        for h in range(chunks):
            rows = pl.ds(pl.multiple_of(owner * slab_own + h * span, span), span)
            copy = pltpu.make_async_copy(
                delta.at[m, rows, :], kept.at[part, pl.ds(h * span, span), :], sems.at[part, h]
            )
            copy.start()
            copies.append(copy)
    return copies


def owners_of(chip, core):
    return [(m, chip * CORES + core) for m in range(2)]


def wait_for(copies, part, chunks):
    for copy in copies[part * chunks : (part + 1) * chunks]:
        copy.wait()


def early_kernel(
    place, scale_num, mask_hbm, own, sib, delta, theirs, kept, held, mask, sems, mask_sem
):
    chip, core = place[0], place[1]
    chunks = sems.shape[1]
    mask_copy = pltpu.make_async_copy(mask_hbm, mask, mask_sem)
    mask_copy.start()
    owners = owners_of(1 - chip, 1 - core) + owners_of(1 - chip, core)
    copies = fetch(delta, kept, sems, owners, chunks)
    gather_held(held, (own, sib))
    scale = scale_num[0].astype(jnp.float32) / DEN
    mask_copy.wait()
    for part, (m, owner) in enumerate(owners[:2]):
        wait_for(copies, part, chunks)
        total = scale * dot_rows(held[...], kept_blocks(mask, kept.at[part], m, owner))
        put(half_of(theirs, m), total, core)
    for part in (2, 3):
        wait_for(copies, part, chunks)


def early_rest_kernel(place, scale_num, mask, own, sib, kept, ours, held):
    chip, core = place[0], place[1]
    gather_held(held, (own, sib))
    scale = scale_num[0].astype(jnp.float32) / DEN
    for part, (m, owner) in enumerate(owners_of(1 - chip, core)):
        total = scale * dot_rows(held[...], kept_blocks(mask, kept.at[2 + part], m, owner))
        put(half_of(ours, m), total, core)


def later_kernel(
    place, scale_num, mask, own, sib, far_own, far_sib, kept, delta, theirs, ours, theirs_home,
    home, held, sems,
):
    chip, core = place[0], place[1]
    chunks = sems.shape[1]
    half = held.shape[0] // 2
    home_owners = owners_of(chip, 1 - core)
    copies = fetch(delta, home, sems, home_owners, chunks)
    gather_held(held, (own, sib, far_own, far_sib))
    scale = scale_num[0].astype(jnp.float32) / DEN
    owners = owners_of(1 - chip, 1 - core) + owners_of(1 - chip, core)
    for part, (m, owner) in enumerate(owners):
        total = scale * dot_rows(held[half:], kept_blocks(mask, kept.at[part], m, owner))
        put(half_of(theirs if part < 2 else ours, m), total, core)
    for part, (m, owner) in enumerate(home_owners):
        wait_for(copies, part, chunks)
        total = scale * dot_rows(held[...], kept_blocks(mask, home.at[part], m, owner))
        put(half_of(theirs_home, m), total, core)


def home_kernel(
    place, scale_num, mask, own, sib, far_own, far_sib, delta, base, ours,
    kept, kept_base, held, sems, base_sems,
):
    chip, core = place[0], place[1]
    chunks = sems.shape[1]
    owners = owners_of(chip, core)
    copies = fetch(delta, kept, sems, owners, chunks)
    base_copies = fetch(base, kept_base, base_sems, [(0, 0), (1, 0)], chunks)
    gather_held(held, (own, sib, far_own, far_sib))
    scale = scale_num[0].astype(jnp.float32) / DEN
    for part, (m, owner) in enumerate(owners):
        wait_for(copies, part, chunks)
        total = scale * dot_rows(held[...], kept_blocks(mask, kept.at[part], m, owner))
        wait_for(base_copies, part, chunks)
        put(half_of(ours, m), total + dot_rows(held[...], kept_base[part]), core)


def call(kernel, outs, scratch, in_specs, operands, flops, traffic):
    return pl.pallas_call(
        kernel,
        out_shape=outs,
        in_specs=in_specs,
        out_specs=[VMEM] * len(outs),
        scratch_shapes=scratch,
        compiler_params=pltpu.CompilerParams(vmem_limit_bytes=50 * MIB),
        cost_estimate=pl.CostEstimate(flops=flops // 8, bytes_accessed=traffic // 8, transcendentals=0),
    )(*operands)


def join_kernel(ours, arrived, out):
    out[...] = (ours[...] + arrived[...].astype(jnp.float32)).astype(out.dtype)


def join_home_kernel(ours, arrived, near, far, out):
    for x, other in enumerate((near, far)):
        total = ours[:, x] + arrived[:, x].astype(jnp.float32) + other[...].astype(jnp.float32)
        out[:, x] = total.astype(out.dtype)


def last_kernel(place, parts, out, total):
    chip, core = place[0], place[1]
    rows = parts.shape[-2]
    slab_own = out.shape[1]
    for x in range(2):
        at = chip if x == 0 else 1 - chip
        for c in range(CORES):
            both = jnp.sum(parts[:, x, c].astype(jnp.float32), axis=0)
            value = silu_times(both[:, :slab_own], both[:, slab_own:])
            total[pl.ds(pl.multiple_of((at * CORES + c) * rows, rows), rows), :] = value
    out[...] = total[...].astype(out.dtype)


def local_pair(delta, drop_mask, scale_num, base, tokens, *, groups):
    rows, width = tokens.shape[0], tokens.shape[1] // groups
    slab_own = base.shape[1]
    f32, bf16 = jnp.float32, jnp.bfloat16
    me = lax.axis_index("ckpt")
    place = jnp.stack([me >> 1, me & 1]).astype(jnp.int32)
    mask, delta = drop_mask[0], delta[0]
    mask_hbm = pltpu.with_memory_space_constraint(mask, pltpu.HBM)
    core_swap = functools.partial(lax.ppermute, axis_name="ckpt", perm=[(i, i ^ 1) for i in range(4)])
    chip_swap = functools.partial(lax.ppermute, axis_name="ckpt", perm=[(i, i ^ 2) for i in range(4)])

    cut = tokens.reshape(rows, groups, width).transpose(1, 0, 2)
    own = lax.all_to_all(cut, "tensor", 0, 0, tiled=True).reshape(groups * rows, width)
    far_own = chip_swap(own)
    sib = core_swap(own)

    half = groups * rows * CORES
    chunks = 2
    part = jax.ShapeDtypeStruct
    pair = (groups, CORES, rows, 2 * slab_own)
    four = (groups, 2, CORES, rows, 2 * slab_own)
    weights = (4, slab_own, width)
    size = 4 * slab_own * width
    theirs, kept = call(
        early_kernel,
        [part(pair, bf16), part(weights, bf16)],
        [
            pltpu.VMEM((half, width), bf16),
            pltpu.SMEM(mask.shape, mask.dtype),
            pltpu.SemaphoreType.DMA((4, chunks)),
            pltpu.SemaphoreType.DMA(()),
        ],
        [SMEM, SMEM, HBM, VMEM, VMEM, HBM],
        (place, scale_num, mask_hbm, own, sib, delta),
        half * size,
        2 * size,
    )
    near = core_swap(theirs)
    (ours,) = call(
        early_rest_kernel,
        [part(pair, f32)],
        [pltpu.VMEM((half, width), bf16)],
        [SMEM, SMEM, SMEM, VMEM, VMEM, VMEM],
        (place, scale_num, mask, own, sib, kept),
        half * size,
        size,
    )
    far_own, ours = lax.optimization_barrier((far_own, ours))
    far_sib = core_swap(far_own)
    simple = lambda kernel, shape, *xs: pl.pallas_call(
        kernel,
        out_shape=part(shape, bf16),
        in_specs=[VMEM] * len(xs),
        out_specs=VMEM,
        compiler_params=pltpu.CompilerParams(vmem_limit_bytes=16 * MIB),
        cost_estimate=pl.CostEstimate(flops=xs[0].size, bytes_accessed=8 * xs[0].size, transcendentals=0),
    )(*xs)
    first, far_sib = lax.optimization_barrier((simple(join_kernel, pair, ours, near), far_sib))
    over_first = chip_swap(first)
    theirs, ours, theirs_home = call(
        later_kernel,
        [part(pair, bf16), part(pair, f32), part(four, bf16)],
        [
            pltpu.VMEM((2, slab_own, width), bf16),
            pltpu.VMEM((2 * half, width), bf16),
            pltpu.SemaphoreType.DMA((2, chunks)),
        ],
        [SMEM, SMEM, SMEM, VMEM, VMEM, VMEM, VMEM, VMEM, HBM],
        (place, scale_num, mask, own, sib, far_own, far_sib, kept, delta),
        4 * half * size,
        2 * size,
    )
    theirs, theirs_home, over_first = lax.optimization_barrier((theirs, theirs_home, over_first))
    second = simple(join_kernel, pair, ours, core_swap(theirs))
    near_home = core_swap(theirs_home)
    second, own = lax.optimization_barrier((second, own))
    over_second = chip_swap(second)
    (ours,) = call(
        home_kernel,
        [part(four, f32)],
        [
            pltpu.VMEM((2, slab_own, width), bf16),
            pltpu.VMEM((2, slab_own, width), bf16),
            pltpu.VMEM((2 * half, width), bf16),
            pltpu.SemaphoreType.DMA((2, chunks)),
            pltpu.SemaphoreType.DMA((2, chunks)),
        ],
        [SMEM, SMEM, SMEM, VMEM, VMEM, VMEM, VMEM, HBM, HBM],
        (place, scale_num, mask, own, sib, far_own, far_sib, delta, base),
        4 * half * size,
        2 * size,
    )
    whole = simple(join_home_kernel, four, ours, near_home, over_second, over_first)
    parts = lax.all_to_all(whole, "tensor", 0, 0, tiled=True)
    return pl.pallas_call(
        last_kernel,
        out_shape=part((2 * CORES * rows, slab_own), bf16),
        in_specs=[SMEM, VMEM],
        out_specs=VMEM,
        scratch_shapes=[pltpu.VMEM((2 * CORES * rows, slab_own), f32)],
        compiler_params=pltpu.CompilerParams(vmem_limit_bytes=16 * MIB),
    )(place, parts)


def masked_rows(mask_ref, delta_ref, kept, m, row_block):
    for i in range(kept.shape[0] // BLOCK):
        for j in range(kept.shape[1] // BLOCK):
            keep = mask_ref[m, row_block * (kept.shape[0] // BLOCK) + i, j] != 0
            here = (slice(i * BLOCK, (i + 1) * BLOCK), slice(j * BLOCK, (j + 1) * BLOCK))
            piece = delta_ref[0, here[0], here[1]]
            kept[here] = jnp.where(keep, piece, jnp.zeros_like(piece))


def partial_kernel(with_base, rows, place_ref, scale_ref, mask_ref, own_ref, sib_ref, delta_ref, *rest):
    if with_base:
        base_ref, out_ref, held, kept = rest
    else:
        out_ref, held, kept = rest
    row, core = place_ref[0], place_ref[1]
    target = place_ref[2]
    step, m = pl.program_id(0), pl.program_id(1)

    @pl.when((step == 0) & (m == 0))
    def _():
        half = own_ref.shape[0]
        held[:half] = own_ref[...]
        held[half:] = sib_ref[...]

    masked_rows(mask_ref, delta_ref, kept, m, step * CORES + target)
    scale = scale_ref[0].astype(jnp.float32) / DEN

    def store(total):
        groups = out_ref.shape[1]
        split = total.reshape(CORES, -1, groups, rows, total.shape[-1])
        span = split.shape[1] * rows
        for side, at in ((0, core), (1, 1 - core)):
            for g in range(groups):
                piece = split[side, :, g].reshape(span, -1).astype(out_ref.dtype)
                out_ref[0, g, pl.ds(pl.multiple_of(at * span, span), span), :] = piece

    product = scale * dot_rows(held[...], kept[...])
    if with_base:

        @pl.when(step == row)
        def _():
            store(product + dot_rows(held[...], base_ref[0]))

        @pl.when(step != row)
        def _():
            store(product)

    else:
        store(product)


def partials(place, scale_num, mask, own, sib, delta, base, slab_own, groups, rows):
    width = delta.shape[2]
    owners = delta.shape[1] // slab_own // CORES
    span = 2 * own.shape[0] // groups
    whole = lambda *_: (0, 0)
    in_specs = [
        pl.BlockSpec(own.shape, whole),
        pl.BlockSpec(sib.shape, whole),
        pl.BlockSpec((1, slab_own, width), lambda x, m, place, *_: (m, x * CORES + place[2], 0)),
    ]
    operands = [own, sib, delta]
    if base is not None:
        in_specs.append(pl.BlockSpec((1, slab_own, width), lambda x, m, *_: (m, 0, 0)))
        operands.append(base)
    out_dtype = jnp.bfloat16 if base is None else jnp.float32
    flops = 2 * 2 * own.shape[0] * width * 2 * slab_own * owners
    return pl.pallas_call(
        functools.partial(partial_kernel, base is not None, rows),
        out_shape=jax.ShapeDtypeStruct((owners, groups, span, 2 * slab_own), out_dtype),
        grid_spec=pltpu.PrefetchScalarGridSpec(
            num_scalar_prefetch=3,
            grid=(owners, 2),
            in_specs=in_specs,
            out_specs=pl.BlockSpec((1, groups, span, slab_own), lambda x, m, *_: (x, 0, 0, m)),
            scratch_shapes=[
                pltpu.VMEM((2 * own.shape[0], width), jnp.bfloat16),
                pltpu.VMEM((slab_own, width), jnp.bfloat16),
            ],
        ),
        compiler_params=pltpu.CompilerParams(vmem_limit_bytes=40 * MIB),
        cost_estimate=pl.CostEstimate(
            flops=flops, bytes_accessed=2 * slab_own * owners * width * 2, transcendentals=0
        ),
    )(place, scale_num, mask, *operands)


def finish_kernel(rows, part_ref, out_ref, total):
    step = pl.program_id(0)
    here = jnp.sum(part_ref[...].astype(jnp.float32), axis=0)

    @pl.when(step == 0)
    def _():
        total[...] = here

    @pl.when(step != 0)
    def _():
        total[...] += here

    @pl.when(step == pl.num_programs(0) - 1)
    def _():
        slab_own = out_ref.shape[1]
        value = silu_times(total[:, :slab_own], total[:, slab_own:])
        split = value.reshape(CORES, -1, rows, slab_own)
        pieces = [split[core, x] for x in range(split.shape[1]) for core in range(CORES)]
        out_ref[...] = jnp.concatenate(pieces, axis=0).astype(out_ref.dtype)


def finish(parts, rows):
    sources, span, both = parts.shape
    block = min(sources, 16)
    return pl.pallas_call(
        functools.partial(finish_kernel, rows),
        out_shape=jax.ShapeDtypeStruct((span, both // 2), jnp.bfloat16),
        grid=(sources // block,),
        in_specs=[pl.BlockSpec((block, span, both), lambda i: (i, 0, 0))],
        out_specs=pl.BlockSpec((span, both // 2), lambda i: (0, 0)),
        scratch_shapes=[pltpu.VMEM((span, both), jnp.float32)],
        compiler_params=pltpu.CompilerParams(vmem_limit_bytes=32 * MIB),
        cost_estimate=pl.CostEstimate(
            flops=parts.size, bytes_accessed=2 * parts.size, transcendentals=span * both // 2
        ),
    )(parts)


def local_any(delta, drop_mask, scale_num, base, tokens, *, ckpts, groups):
    owners = ckpts // CORES
    both = ("ckpt", "tensor")
    same_core = [
        [(x * CORES + core) * groups + t for x in range(owners) for t in range(groups)]
        for core in range(CORES)
    ]
    swap = [(i, i ^ 1) for i in range(ckpts)]
    rows, width = tokens.shape
    width //= groups
    slab_own = base.shape[1]
    me = lax.axis_index("ckpt")
    row, core = me // CORES, me % CORES

    cut = tokens.reshape(rows, groups, width).transpose(1, 0, 2)
    send = jnp.broadcast_to(cut[None], (owners, groups, rows, width)).reshape(-1, rows, width)
    own = lax.all_to_all(send, both, 0, 0, axis_index_groups=same_core, tiled=True)
    own = own.reshape(owners * groups * rows, width)
    sib = lax.ppermute(own, "ckpt", swap)

    common = (own, sib, delta[0])
    place = jnp.stack([row, core, 1 - core]).astype(jnp.int32)
    theirs = partials(place, scale_num, drop_mask[0], *common, None, slab_own, groups, rows)
    arrived = lax.ppermute(theirs, "ckpt", swap)
    place = jnp.stack([row, core, core]).astype(jnp.int32)
    ours = partials(place, scale_num, drop_mask[0], *common, base, slab_own, groups, rows)
    chip = (ours + arrived.astype(jnp.float32)).astype(jnp.bfloat16)
    chip = chip.reshape(owners * groups, -1, 2 * slab_own)
    parts = lax.all_to_all(chip, both, 0, 0, axis_index_groups=same_core, tiled=True)
    return finish(parts, rows)


def solution(mesh):
    ckpts, groups = mesh.shape["ckpt"], mesh.shape["tensor"]
    if ckpts == 2 * CORES:
        local = functools.partial(local_pair, groups=groups)
    else:
        local = functools.partial(local_any, ckpts=ckpts, groups=groups)
    in_specs = (
        P("ckpt", None, None, "tensor"),
        P("ckpt", None, None, "tensor"),
        P("ckpt"),
        P(None, "ckpt", "tensor"),
        P(("tensor", "ckpt"), None),
    )
    out_specs = P("tensor", "ckpt")
    return jax.shard_map(local, mesh=mesh, in_specs=in_specs, out_specs=out_specs, check_vma=False)
```

```python
import functools

import jax
import jax.numpy as jnp
from jax import lax
from jax.experimental import pallas as pl
from jax.experimental.pallas import tpu as pltpu
from jax.sharding import PartitionSpec as P

BLOCK = 128
DEN = 16
CORES = 2
MIB = 1 << 20
VMEM = pl.BlockSpec(memory_space=pltpu.VMEM)
SMEM = pl.BlockSpec(memory_space=pltpu.SMEM)
HBM = pl.BlockSpec(memory_space=pltpu.HBM)


def dot_rows(tokens, weights):
    return lax.dot_general(
        tokens, weights, (((1,), (1,)), ((), ())), preferred_element_type=jnp.float32
    )


def silu_times(gate, up):
    return gate / (1 + jnp.exp(-gate)) * up


def gather_held(held, pieces):
    for i, piece in enumerate(pieces):
        span = piece.shape[0]
        held[i * span : (i + 1) * span] = piece[...]


def expand(mask, scale, factors):
    blocks, width = mask.shape[-1], factors.shape[1]
    column = lax.broadcasted_iota(jnp.int32, (blocks, width), 1) // BLOCK
    row = lax.broadcasted_iota(jnp.int32, (blocks, width), 0)
    spread = jnp.where(column == row, 1.0, 0.0).astype(jnp.float32)
    kept = jnp.where(mask.reshape(-1, blocks) != 0, scale, 0.0).astype(jnp.float32)
    factors[...] = jnp.dot(kept, spread, preferred_element_type=jnp.float32)


def terms(factors, weights, m, owner):
    strips = weights.shape[0] // BLOCK
    first = m * (factors.shape[0] // 2) + owner * strips
    scaled = []
    for i in range(strips):
        factor = factors[pl.ds(first + i, 1), :].astype(weights.dtype)
        scaled.append(weights[i * BLOCK : (i + 1) * BLOCK] * factor)
    return jnp.concatenate(scaled, axis=0)


def chip_and_core():
    me = lax.axis_index("ckpt")
    return me >> 1, me & 1


def put(view, total, core):
    groups, rows = view.shape[-5 if len(view.shape) == 5 else 0], view.shape[-2]
    split = total.reshape(-1, CORES, groups, rows, total.shape[-1])
    for x in range(split.shape[0]):
        for side in range(CORES):
            at = core if side == 0 else 1 - core
            for g in range(groups):
                here = (g, at) if len(view.shape) == 4 else (g, x, at)
                view[here] = split[x, side, g].astype(view.dtype)


def half_of(ref, m):
    size = ref.shape[-1] // 2
    return ref.at[(slice(None),) * (len(ref.shape) - 1) + (slice(m * size, (m + 1) * size),)]


def fetch(delta, kept, sems, owners, chunks):
    slab_own = kept.shape[1]
    span = slab_own // chunks
    copies = []
    for part, (m, owner) in enumerate(owners):
        for h in range(chunks):
            rows = pl.ds(pl.multiple_of(owner * slab_own + h * span, span), span)
            copy = pltpu.make_async_copy(
                delta.at[m, rows, :], kept.at[part, pl.ds(h * span, span), :], sems.at[part, h]
            )
            copy.start()
            copies.append(copy)
    return copies


def owners_of(chip, core):
    return [(m, chip * CORES + core) for m in range(2)]


def wait_for(copies, part, chunks):
    for copy in copies[part * chunks : (part + 1) * chunks]:
        copy.wait()


def early_kernel(
    scale_num, mask_hbm, own, sib, delta, theirs, kept, factors, held, mask, sems, mask_sem
):
    chip, core = chip_and_core()
    chunks = sems.shape[1]
    mask_copy = pltpu.make_async_copy(mask_hbm, mask, mask_sem)
    mask_copy.start()
    owners = owners_of(1 - chip, 1 - core) + owners_of(1 - chip, core)
    copies = fetch(delta, kept, sems, owners, chunks)
    gather_held(held, (own, sib))
    mask_copy.wait()
    expand(mask[...], scale_num[0].astype(jnp.float32) / DEN, factors)
    for part, (m, owner) in enumerate(owners[:2]):
        wait_for(copies, part, chunks)
        total = dot_rows(held[...], terms(factors, kept.at[part], m, owner))
        put(half_of(theirs, m), total, core)
    for part in (2, 3):
        wait_for(copies, part, chunks)


def early_rest_kernel(factors, own, sib, kept, ours, held):
    chip, core = chip_and_core()
    gather_held(held, (own, sib))
    for part, (m, owner) in enumerate(owners_of(1 - chip, core)):
        total = dot_rows(held[...], terms(factors, kept.at[2 + part], m, owner))
        put(half_of(ours, m), total, core)


def later_kernel(
    factors, own, sib, far_own, far_sib, kept, delta, theirs, ours, theirs_home, home, held, sems
):
    chip, core = chip_and_core()
    chunks = sems.shape[1]
    half = held.shape[0] // 2
    home_owners = owners_of(chip, 1 - core)
    copies = fetch(delta, home, sems, home_owners, chunks)
    gather_held(held, (own, sib, far_own, far_sib))
    owners = owners_of(1 - chip, 1 - core) + owners_of(1 - chip, core)
    for part, (m, owner) in enumerate(owners):
        total = dot_rows(held[half:], terms(factors, kept.at[part], m, owner))
        put(half_of(theirs if part < 2 else ours, m), total, core)
    for part, (m, owner) in enumerate(home_owners):
        wait_for(copies, part, chunks)
        total = dot_rows(held[...], terms(factors, home.at[part], m, owner))
        put(half_of(theirs_home, m), total, core)


def home_kernel(
    factors, own, sib, far_own, far_sib, delta, base, ours, kept, kept_base, held, sems, base_sems
):
    chip, core = chip_and_core()
    chunks = sems.shape[1]
    owners = owners_of(chip, core)
    copies = fetch(delta, kept, sems, owners, chunks)
    base_copies = fetch(base, kept_base, base_sems, [(0, 0), (1, 0)], chunks)
    gather_held(held, (own, sib, far_own, far_sib))
    for part, (m, owner) in enumerate(owners):
        wait_for(copies, part, chunks)
        total = dot_rows(held[...], terms(factors, kept.at[part], m, owner))
        wait_for(base_copies, part, chunks)
        put(half_of(ours, m), total + dot_rows(held[...], kept_base[part]), core)


def call(kernel, outs, scratch, in_specs, operands, flops, traffic):
    return pl.pallas_call(
        kernel,
        out_shape=outs,
        in_specs=in_specs,
        out_specs=[VMEM] * len(outs),
        scratch_shapes=scratch,
        compiler_params=pltpu.CompilerParams(vmem_limit_bytes=50 * MIB),
        cost_estimate=pl.CostEstimate(flops=flops // 8, bytes_accessed=traffic // 8, transcendentals=0),
    )(*operands)


def join_kernel(ours, arrived, out):
    out[...] = (ours[...] + arrived[...].astype(jnp.float32)).astype(out.dtype)


def join_home_kernel(ours, arrived, near, far, out):
    for x, other in enumerate((near, far)):
        total = ours[:, x] + arrived[:, x].astype(jnp.float32) + other[...].astype(jnp.float32)
        out[:, x] = total.astype(out.dtype)


def last_kernel(parts, out, total):
    chip, _ = chip_and_core()
    rows = parts.shape[-2]
    slab_own = out.shape[1]
    for x in range(2):
        at = chip if x == 0 else 1 - chip
        for c in range(CORES):
            both = jnp.sum(parts[:, x, c].astype(jnp.float32), axis=0)
            value = silu_times(both[:, :slab_own], both[:, slab_own:])
            total[pl.ds(pl.multiple_of((at * CORES + c) * rows, rows), rows), :] = value
    out[...] = total[...].astype(out.dtype)


def local_pair(delta, drop_mask, scale_num, base, tokens, *, groups):
    rows, width = tokens.shape[0], tokens.shape[1] // groups
    slab_own = base.shape[1]
    f32, bf16 = jnp.float32, jnp.bfloat16
    mask, delta = drop_mask[0], delta[0]
    core_swap = functools.partial(lax.ppermute, axis_name="ckpt", perm=[(i, i ^ 1) for i in range(4)])
    chip_swap = functools.partial(lax.ppermute, axis_name="ckpt", perm=[(i, i ^ 2) for i in range(4)])

    cut = tokens.reshape(rows, groups, width).transpose(1, 0, 2)
    own = lax.all_to_all(cut, "tensor", 0, 0, tiled=True).reshape(groups * rows, width)
    far_own = chip_swap(own)
    sib = core_swap(own)

    half = groups * rows * CORES
    chunks = 2
    part = jax.ShapeDtypeStruct
    pair = (groups, CORES, rows, 2 * slab_own)
    four = (groups, 2, CORES, rows, 2 * slab_own)
    weights = (4, slab_own, width)
    size = 4 * slab_own * width
    theirs, kept, factors = call(
        early_kernel,
        [part(pair, bf16), part(weights, bf16), part((mask.shape[0] * mask.shape[1], width), f32)],
        [
            pltpu.VMEM((half, width), bf16),
            pltpu.VMEM(mask.shape, mask.dtype),
            pltpu.SemaphoreType.DMA((4, chunks)),
            pltpu.SemaphoreType.DMA(()),
        ],
        [SMEM, HBM, VMEM, VMEM, HBM],
        (scale_num, pltpu.with_memory_space_constraint(mask, pltpu.HBM), own, sib, delta),
        half * size,
        2 * size,
    )
    near = core_swap(theirs)
    (ours,) = call(
        early_rest_kernel,
        [part(pair, f32)],
        [pltpu.VMEM((half, width), bf16)],
        [VMEM] * 4,
        (factors, own, sib, kept),
        half * size,
        size,
    )
    far_own, ours = lax.optimization_barrier((far_own, ours))
    far_sib = core_swap(far_own)
    simple = lambda kernel, shape, *xs: pl.pallas_call(
        kernel,
        out_shape=part(shape, bf16),
        in_specs=[VMEM] * len(xs),
        out_specs=VMEM,
        compiler_params=pltpu.CompilerParams(vmem_limit_bytes=16 * MIB),
        cost_estimate=pl.CostEstimate(flops=xs[0].size, bytes_accessed=8 * xs[0].size, transcendentals=0),
    )(*xs)
    first, far_sib = lax.optimization_barrier((simple(join_kernel, pair, ours, near), far_sib))
    over_first = chip_swap(first)
    theirs, ours, theirs_home = call(
        later_kernel,
        [part(pair, bf16), part(pair, f32), part(four, bf16)],
        [
            pltpu.VMEM((2, slab_own, width), bf16),
            pltpu.VMEM((2 * half, width), bf16),
            pltpu.SemaphoreType.DMA((2, chunks)),
        ],
        [VMEM] * 6 + [HBM],
        (factors, own, sib, far_own, far_sib, kept, delta),
        4 * half * size,
        2 * size,
    )
    theirs, theirs_home, over_first = lax.optimization_barrier((theirs, theirs_home, over_first))
    second = simple(join_kernel, pair, ours, core_swap(theirs))
    near_home = core_swap(theirs_home)
    second, own = lax.optimization_barrier((second, own))
    over_second = chip_swap(second)
    (ours,) = call(
        home_kernel,
        [part(four, f32)],
        [
            pltpu.VMEM((2, slab_own, width), bf16),
            pltpu.VMEM((2, slab_own, width), bf16),
            pltpu.VMEM((2 * half, width), bf16),
            pltpu.SemaphoreType.DMA((2, chunks)),
            pltpu.SemaphoreType.DMA((2, chunks)),
        ],
        [VMEM] * 5 + [HBM, HBM],
        (factors, own, sib, far_own, far_sib, delta, base),
        4 * half * size,
        2 * size,
    )
    whole = simple(join_home_kernel, four, ours, near_home, over_second, over_first)
    parts = lax.all_to_all(whole, "tensor", 0, 0, tiled=True)
    return pl.pallas_call(
        last_kernel,
        out_shape=part((2 * CORES * rows, slab_own), bf16),
        in_specs=[VMEM],
        out_specs=VMEM,
        scratch_shapes=[pltpu.VMEM((2 * CORES * rows, slab_own), f32)],
        compiler_params=pltpu.CompilerParams(vmem_limit_bytes=16 * MIB),
    )(parts)


def masked_rows(mask_ref, delta_ref, kept, m, row_block):
    for i in range(kept.shape[0] // BLOCK):
        for j in range(kept.shape[1] // BLOCK):
            keep = mask_ref[m, row_block * (kept.shape[0] // BLOCK) + i, j] != 0
            here = (slice(i * BLOCK, (i + 1) * BLOCK), slice(j * BLOCK, (j + 1) * BLOCK))
            piece = delta_ref[0, here[0], here[1]]
            kept[here] = jnp.where(keep, piece, jnp.zeros_like(piece))


def partial_kernel(with_base, rows, place_ref, scale_ref, mask_ref, own_ref, sib_ref, delta_ref, *rest):
    if with_base:
        base_ref, out_ref, held, kept = rest
    else:
        out_ref, held, kept = rest
    row, core = place_ref[0], place_ref[1]
    target = place_ref[2]
    step, m = pl.program_id(0), pl.program_id(1)

    @pl.when((step == 0) & (m == 0))
    def _():
        half = own_ref.shape[0]
        held[:half] = own_ref[...]
        held[half:] = sib_ref[...]

    masked_rows(mask_ref, delta_ref, kept, m, step * CORES + target)
    scale = scale_ref[0].astype(jnp.float32) / DEN

    def store(total):
        groups = out_ref.shape[1]
        split = total.reshape(CORES, -1, groups, rows, total.shape[-1])
        span = split.shape[1] * rows
        for side, at in ((0, core), (1, 1 - core)):
            for g in range(groups):
                piece = split[side, :, g].reshape(span, -1).astype(out_ref.dtype)
                out_ref[0, g, pl.ds(pl.multiple_of(at * span, span), span), :] = piece

    product = scale * dot_rows(held[...], kept[...])
    if with_base:

        @pl.when(step == row)
        def _():
            store(product + dot_rows(held[...], base_ref[0]))

        @pl.when(step != row)
        def _():
            store(product)

    else:
        store(product)


def partials(place, scale_num, mask, own, sib, delta, base, slab_own, groups, rows):
    width = delta.shape[2]
    owners = delta.shape[1] // slab_own // CORES
    span = 2 * own.shape[0] // groups
    whole = lambda *_: (0, 0)
    in_specs = [
        pl.BlockSpec(own.shape, whole),
        pl.BlockSpec(sib.shape, whole),
        pl.BlockSpec((1, slab_own, width), lambda x, m, place, *_: (m, x * CORES + place[2], 0)),
    ]
    operands = [own, sib, delta]
    if base is not None:
        in_specs.append(pl.BlockSpec((1, slab_own, width), lambda x, m, *_: (m, 0, 0)))
        operands.append(base)
    out_dtype = jnp.bfloat16 if base is None else jnp.float32
    flops = 2 * 2 * own.shape[0] * width * 2 * slab_own * owners
    return pl.pallas_call(
        functools.partial(partial_kernel, base is not None, rows),
        out_shape=jax.ShapeDtypeStruct((owners, groups, span, 2 * slab_own), out_dtype),
        grid_spec=pltpu.PrefetchScalarGridSpec(
            num_scalar_prefetch=3,
            grid=(owners, 2),
            in_specs=in_specs,
            out_specs=pl.BlockSpec((1, groups, span, slab_own), lambda x, m, *_: (x, 0, 0, m)),
            scratch_shapes=[
                pltpu.VMEM((2 * own.shape[0], width), jnp.bfloat16),
                pltpu.VMEM((slab_own, width), jnp.bfloat16),
            ],
        ),
        compiler_params=pltpu.CompilerParams(vmem_limit_bytes=40 * MIB),
        cost_estimate=pl.CostEstimate(
            flops=flops, bytes_accessed=2 * slab_own * owners * width * 2, transcendentals=0
        ),
    )(place, scale_num, mask, *operands)


def finish_kernel(rows, part_ref, out_ref, total):
    step = pl.program_id(0)
    here = jnp.sum(part_ref[...].astype(jnp.float32), axis=0)

    @pl.when(step == 0)
    def _():
        total[...] = here

    @pl.when(step != 0)
    def _():
        total[...] += here

    @pl.when(step == pl.num_programs(0) - 1)
    def _():
        slab_own = out_ref.shape[1]
        value = silu_times(total[:, :slab_own], total[:, slab_own:])
        split = value.reshape(CORES, -1, rows, slab_own)
        pieces = [split[core, x] for x in range(split.shape[1]) for core in range(CORES)]
        out_ref[...] = jnp.concatenate(pieces, axis=0).astype(out_ref.dtype)


def finish(parts, rows):
    sources, span, both = parts.shape
    block = min(sources, 16)
    return pl.pallas_call(
        functools.partial(finish_kernel, rows),
        out_shape=jax.ShapeDtypeStruct((span, both // 2), jnp.bfloat16),
        grid=(sources // block,),
        in_specs=[pl.BlockSpec((block, span, both), lambda i: (i, 0, 0))],
        out_specs=pl.BlockSpec((span, both // 2), lambda i: (0, 0)),
        scratch_shapes=[pltpu.VMEM((span, both), jnp.float32)],
        compiler_params=pltpu.CompilerParams(vmem_limit_bytes=32 * MIB),
        cost_estimate=pl.CostEstimate(
            flops=parts.size, bytes_accessed=2 * parts.size, transcendentals=span * both // 2
        ),
    )(parts)


def local_any(delta, drop_mask, scale_num, base, tokens, *, ckpts, groups):
    owners = ckpts // CORES
    both = ("ckpt", "tensor")
    same_core = [
        [(x * CORES + core) * groups + t for x in range(owners) for t in range(groups)]
        for core in range(CORES)
    ]
    swap = [(i, i ^ 1) for i in range(ckpts)]
    rows, width = tokens.shape
    width //= groups
    slab_own = base.shape[1]
    me = lax.axis_index("ckpt")
    row, core = me // CORES, me % CORES

    cut = tokens.reshape(rows, groups, width).transpose(1, 0, 2)
    send = jnp.broadcast_to(cut[None], (owners, groups, rows, width)).reshape(-1, rows, width)
    own = lax.all_to_all(send, both, 0, 0, axis_index_groups=same_core, tiled=True)
    own = own.reshape(owners * groups * rows, width)
    sib = lax.ppermute(own, "ckpt", swap)

    common = (own, sib, delta[0])
    place = jnp.stack([row, core, 1 - core]).astype(jnp.int32)
    theirs = partials(place, scale_num, drop_mask[0], *common, None, slab_own, groups, rows)
    arrived = lax.ppermute(theirs, "ckpt", swap)
    place = jnp.stack([row, core, core]).astype(jnp.int32)
    ours = partials(place, scale_num, drop_mask[0], *common, base, slab_own, groups, rows)
    chip = (ours + arrived.astype(jnp.float32)).astype(jnp.bfloat16)
    chip = chip.reshape(owners * groups, -1, 2 * slab_own)
    parts = lax.all_to_all(chip, both, 0, 0, axis_index_groups=same_core, tiled=True)
    return finish(parts, rows)


def solution(mesh):
    ckpts, groups = mesh.shape["ckpt"], mesh.shape["tensor"]
    if ckpts == 2 * CORES:
        local = functools.partial(local_pair, groups=groups)
    else:
        local = functools.partial(local_any, ckpts=ckpts, groups=groups)
    in_specs = (
        P("ckpt", None, None, "tensor"),
        P("ckpt", None, None, "tensor"),
        P("ckpt"),
        P(None, "ckpt", "tensor"),
        P(("tensor", "ckpt"), None),
    )
    out_specs = P("tensor", "ckpt")
    return jax.shard_map(local, mesh=mesh, in_specs=in_specs, out_specs=out_specs, check_vma=False)
```

```python
import functools

import jax
import jax.numpy as jnp
from jax import lax
from jax.experimental import pallas as pl
from jax.experimental.pallas import tpu as pltpu
from jax.sharding import PartitionSpec as P

BLOCK = 128
DEN = 16
CORES = 2
MIB = 1 << 20
VMEM = pl.BlockSpec(memory_space=pltpu.VMEM)
SMEM = pl.BlockSpec(memory_space=pltpu.SMEM)
HBM = pl.BlockSpec(memory_space=pltpu.HBM)


def dot_rows(tokens, weights):
    return lax.dot_general(
        tokens, weights, (((1,), (1,)), ((), ())), preferred_element_type=jnp.float32
    )


def silu_times(gate, up):
    return gate / (1 + jnp.exp(-gate)) * up


def gather_held(held, pieces):
    for i, piece in enumerate(pieces):
        span = piece.shape[0]
        held[i * span : (i + 1) * span] = piece[...]


def expand(mask, scale, factors):
    blocks, width = mask.shape[-1], factors.shape[1]
    column = lax.broadcasted_iota(jnp.int32, (blocks, width), 1) // BLOCK
    row = lax.broadcasted_iota(jnp.int32, (blocks, width), 0)
    spread = jnp.where(column == row, 1.0, 0.0).astype(jnp.float32)
    kept = jnp.where(mask.reshape(-1, blocks) != 0, scale, 0.0).astype(jnp.float32)
    rows = kept.shape[0]
    factors[:rows] = jnp.dot(kept, spread, preferred_element_type=jnp.float32)
    factors[rows:] = jnp.ones((factors.shape[0] - rows, width), jnp.float32)


def product(held, factors, weights, first):
    scaled = []
    for i in range(weights.shape[0] // BLOCK):
        factor = factors[pl.ds(first + i, 1), :].astype(weights.dtype)
        scaled.append(weights[i * BLOCK : (i + 1) * BLOCK] * factor)
    return dot_rows(held, jnp.concatenate(scaled, axis=0))


def chip_and_core():
    me = lax.axis_index("ckpt")
    return me >> 1, me & 1


def put(view, total, core):
    groups, rows = view.shape[0], view.shape[-2]
    split = total.reshape(-1, CORES, groups, rows, total.shape[-1])
    for x in range(split.shape[0]):
        for side in range(CORES):
            at = core if side == 0 else 1 - core
            for g in range(groups):
                here = (g, at) if len(view.shape) == 4 else (g, x, at)
                view[here] = split[x, side, g].astype(view.dtype)


class Rows:
    def __init__(self, source, kept, sems, owners, first=0):
        self.source, self.kept, self.sems, self.owners, self.first = source, kept, sems, owners, first

    def owner(self, part):
        owner = self.owners[0]
        return owner if len(self.owners) == 1 else jnp.where(part < 2, owner, self.owners[1])

    def copies(self, part):
        slab_own, chunks = self.kept.shape[1], self.sems.shape[1]
        span = slab_own // chunks
        at = self.first + part
        for h in range(chunks):
            rows = pl.ds(pl.multiple_of(self.owner(part) * slab_own + h * span, span), span)
            yield pltpu.make_async_copy(
                self.source.at[part % 2, rows, :],
                self.kept.at[at, pl.ds(h * span, span), :],
                self.sems.at[at, h],
            )

    def start(self):
        for part in range(2 * len(self.owners)):
            for copy in self.copies(part):
                copy.start()

    def wait(self, part):
        for copy in self.copies(part):
            copy.wait()


def first_factor(kept, factors, part, owner):
    strips = kept.shape[1] // BLOCK
    blocks = (factors.shape[0] - strips) // 2
    return part % 2 * blocks + owner * strips


def early_kernel(
    scale_num, mask_hbm, own, sib, delta, theirs, ours, kept, factors, held, mask, sems, mask_sem
):
    chip, core = chip_and_core()
    mask_copy = pltpu.make_async_copy(mask_hbm, mask, mask_sem)
    mask_copy.start()
    rows = Rows(delta, kept, sems, [(1 - chip) * CORES + at for at in (1 - core, core)])
    rows.start()
    gather_held(held, (own, sib))
    mask_copy.wait()
    expand(mask[...], scale_num[0].astype(jnp.float32) / DEN, factors)

    @pl.loop(0, 4)
    def _(part):
        rows.wait(part)
        first = first_factor(kept, factors, part, rows.owner(part))
        total = product(held[...], factors, kept.at[part], first)
        pl.when(part < 2)(lambda: put(theirs.at[part % 2], total, core))
        pl.when(part >= 2)(lambda: put(ours.at[part % 2], total, core))


def later_kernel(
    factors, own, sib, far_own, far_sib, kept, delta, theirs, ours, theirs_home, home, held, sems
):
    chip, core = chip_and_core()
    half = held.shape[0] // 2
    rows = Rows(delta, home, sems, [chip * CORES + 1 - core])
    rows.start()
    gather_held(held, (own, sib, far_own, far_sib))
    far = Rows(None, kept, None, [(1 - chip) * CORES + at for at in (1 - core, core)])

    @pl.loop(0, 4)
    def _(part):
        first = first_factor(kept, factors, part, far.owner(part))
        total = product(held[half:], factors, kept.at[part], first)
        pl.when(part < 2)(lambda: put(theirs.at[part % 2], total, core))
        pl.when(part >= 2)(lambda: put(ours.at[part % 2], total, core))

    @pl.loop(0, 2)
    def _(part):
        rows.wait(part)
        first = first_factor(home, factors, part, rows.owner(part))
        put(theirs_home.at[part], product(held[...], factors, home.at[part], first), core)


def home_kernel(factors, own, sib, far_own, far_sib, delta, base, ours, kept, held, total, sems):
    chip, core = chip_and_core()
    rows = Rows(delta, kept, sems, [chip * CORES + core])
    base_rows = Rows(base, kept, sems, [0], first=2)
    rows.start()
    base_rows.start()
    gather_held(held, (own, sib, far_own, far_sib))
    total[...] = jnp.zeros_like(total)
    ones = factors.shape[0] - kept.shape[1] // BLOCK

    @pl.loop(0, 4)
    def _(part):
        pl.when(part < 2)(lambda: rows.wait(part))
        pl.when(part >= 2)(lambda: base_rows.wait(part - 2))
        first = jnp.where(part < 2, first_factor(kept, factors, part, rows.owner(part)), ones)
        total[part % 2] += product(held[...], factors, kept.at[part], first)

    for m in range(2):
        put(ours.at[m], total[m], core)


def call(kernel, outs, scratch, in_specs, operands, flops, traffic):
    return pl.pallas_call(
        kernel,
        out_shape=outs,
        in_specs=in_specs,
        out_specs=[VMEM] * len(outs),
        scratch_shapes=scratch,
        compiler_params=pltpu.CompilerParams(vmem_limit_bytes=50 * MIB),
        cost_estimate=pl.CostEstimate(flops=flops // 8, bytes_accessed=traffic // 8, transcendentals=0),
    )(*operands)


def join_kernel(ours, arrived, out):
    out[...] = (ours[...] + arrived[...].astype(jnp.float32)).astype(out.dtype)


def join_home_kernel(ours, arrived, near, far, out):
    slab_own = ours.shape[-1]
    for m in range(2):
        for x, other in enumerate((near, far)):
            total = ours[m, :, x] + arrived[m, :, x].astype(jnp.float32)
            total = total + other[m].astype(jnp.float32)
            out[:, x, :, :, m * slab_own : (m + 1) * slab_own] = total.astype(out.dtype)


def last_kernel(parts, out, total):
    chip, _ = chip_and_core()
    rows = parts.shape[-2]
    slab_own = out.shape[1]
    for x in range(2):
        at = chip if x == 0 else 1 - chip
        for c in range(CORES):
            both = jnp.sum(parts[:, x, c].astype(jnp.float32), axis=0)
            value = silu_times(both[:, :slab_own], both[:, slab_own:])
            total[pl.ds(pl.multiple_of((at * CORES + c) * rows, rows), rows), :] = value
    out[...] = total[...].astype(out.dtype)


def local_pair(delta, drop_mask, scale_num, base, tokens, *, groups):
    rows, width = tokens.shape[0], tokens.shape[1] // groups
    slab_own = base.shape[1]
    f32, bf16 = jnp.float32, jnp.bfloat16
    mask, delta = drop_mask[0], delta[0]
    core_swap = functools.partial(lax.ppermute, axis_name="ckpt", perm=[(i, i ^ 1) for i in range(4)])
    chip_swap = functools.partial(lax.ppermute, axis_name="ckpt", perm=[(i, i ^ 2) for i in range(4)])

    cut = tokens.reshape(rows, groups, width).transpose(1, 0, 2)
    own = lax.all_to_all(cut, "tensor", 0, 0, tiled=True).reshape(groups * rows, width)
    far_own = chip_swap(own)
    sib = core_swap(own)

    half = groups * rows * CORES
    chunks = 2
    part = jax.ShapeDtypeStruct
    pair = (2, groups, CORES, rows, slab_own)
    four = (2, groups, 2, CORES, rows, slab_own)
    weights = (4, slab_own, width)
    size = 4 * slab_own * width
    blocks = mask.shape[0] * mask.shape[1] + slab_own // BLOCK
    theirs, ours, kept, factors = call(
        early_kernel,
        [part(pair, bf16), part(pair, f32), part(weights, bf16), part((blocks, width), f32)],
        [
            pltpu.VMEM((half, width), bf16),
            pltpu.VMEM(mask.shape, mask.dtype),
            pltpu.SemaphoreType.DMA((4, chunks)),
            pltpu.SemaphoreType.DMA(()),
        ],
        [SMEM, HBM, VMEM, VMEM, HBM],
        (scale_num, pltpu.with_memory_space_constraint(mask, pltpu.HBM), own, sib, delta),
        2 * half * size,
        2 * size,
    )
    near = core_swap(theirs)
    far_own, theirs = lax.optimization_barrier((far_own, theirs))
    far_sib = core_swap(far_own)
    simple = lambda kernel, shape, *xs: pl.pallas_call(
        kernel,
        out_shape=part(shape, bf16),
        in_specs=[VMEM] * len(xs),
        out_specs=VMEM,
        compiler_params=pltpu.CompilerParams(vmem_limit_bytes=16 * MIB),
        cost_estimate=pl.CostEstimate(flops=xs[0].size, bytes_accessed=8 * xs[0].size, transcendentals=0),
    )(*xs)
    first, far_sib = lax.optimization_barrier((simple(join_kernel, pair, ours, near), far_sib))
    over_first = chip_swap(first)
    theirs, ours, theirs_home = call(
        later_kernel,
        [part(pair, bf16), part(pair, f32), part(four, bf16)],
        [
            pltpu.VMEM((2, slab_own, width), bf16),
            pltpu.VMEM((2 * half, width), bf16),
            pltpu.SemaphoreType.DMA((2, chunks)),
        ],
        [VMEM] * 6 + [HBM],
        (factors, own, sib, far_own, far_sib, kept, delta),
        4 * half * size,
        2 * size,
    )
    theirs, theirs_home, over_first = lax.optimization_barrier((theirs, theirs_home, over_first))
    second = simple(join_kernel, pair, ours, core_swap(theirs))
    near_home = core_swap(theirs_home)
    second, own = lax.optimization_barrier((second, own))
    over_second = chip_swap(second)
    (ours,) = call(
        home_kernel,
        [part(four, f32)],
        [
            pltpu.VMEM(weights, bf16),
            pltpu.VMEM((2 * half, width), bf16),
            pltpu.VMEM((2, 2 * half, slab_own), f32),
            pltpu.SemaphoreType.DMA((4, chunks)),
        ],
        [VMEM] * 5 + [HBM, HBM],
        (factors, own, sib, far_own, far_sib, delta, base),
        4 * half * size,
        2 * size,
    )
    whole = simple(
        join_home_kernel, (groups, 2, CORES, rows, 2 * slab_own), ours, near_home, over_second, over_first
    )
    parts = lax.all_to_all(whole, "tensor", 0, 0, tiled=True)
    return pl.pallas_call(
        last_kernel,
        out_shape=part((2 * CORES * rows, slab_own), bf16),
        in_specs=[VMEM],
        out_specs=VMEM,
        scratch_shapes=[pltpu.VMEM((2 * CORES * rows, slab_own), f32)],
        compiler_params=pltpu.CompilerParams(vmem_limit_bytes=16 * MIB),
    )(parts)


def masked_rows(mask_ref, delta_ref, kept, m, row_block):
    for i in range(kept.shape[0] // BLOCK):
        for j in range(kept.shape[1] // BLOCK):
            keep = mask_ref[m, row_block * (kept.shape[0] // BLOCK) + i, j] != 0
            here = (slice(i * BLOCK, (i + 1) * BLOCK), slice(j * BLOCK, (j + 1) * BLOCK))
            piece = delta_ref[0, here[0], here[1]]
            kept[here] = jnp.where(keep, piece, jnp.zeros_like(piece))


def partial_kernel(with_base, rows, place_ref, scale_ref, mask_ref, own_ref, sib_ref, delta_ref, *rest):
    if with_base:
        base_ref, out_ref, held, kept = rest
    else:
        out_ref, held, kept = rest
    row, core = place_ref[0], place_ref[1]
    target = place_ref[2]
    step, m = pl.program_id(0), pl.program_id(1)

    @pl.when((step == 0) & (m == 0))
    def _():
        half = own_ref.shape[0]
        held[:half] = own_ref[...]
        held[half:] = sib_ref[...]

    masked_rows(mask_ref, delta_ref, kept, m, step * CORES + target)
    scale = scale_ref[0].astype(jnp.float32) / DEN

    def store(total):
        groups = out_ref.shape[1]
        split = total.reshape(CORES, -1, groups, rows, total.shape[-1])
        span = split.shape[1] * rows
        for side, at in ((0, core), (1, 1 - core)):
            for g in range(groups):
                piece = split[side, :, g].reshape(span, -1).astype(out_ref.dtype)
                out_ref[0, g, pl.ds(pl.multiple_of(at * span, span), span), :] = piece

    product = scale * dot_rows(held[...], kept[...])
    if with_base:

        @pl.when(step == row)
        def _():
            store(product + dot_rows(held[...], base_ref[0]))

        @pl.when(step != row)
        def _():
            store(product)

    else:
        store(product)


def partials(place, scale_num, mask, own, sib, delta, base, slab_own, groups, rows):
    width = delta.shape[2]
    owners = delta.shape[1] // slab_own // CORES
    span = 2 * own.shape[0] // groups
    whole = lambda *_: (0, 0)
    in_specs = [
        pl.BlockSpec(own.shape, whole),
        pl.BlockSpec(sib.shape, whole),
        pl.BlockSpec((1, slab_own, width), lambda x, m, place, *_: (m, x * CORES + place[2], 0)),
    ]
    operands = [own, sib, delta]
    if base is not None:
        in_specs.append(pl.BlockSpec((1, slab_own, width), lambda x, m, *_: (m, 0, 0)))
        operands.append(base)
    out_dtype = jnp.bfloat16 if base is None else jnp.float32
    flops = 2 * 2 * own.shape[0] * width * 2 * slab_own * owners
    return pl.pallas_call(
        functools.partial(partial_kernel, base is not None, rows),
        out_shape=jax.ShapeDtypeStruct((owners, groups, span, 2 * slab_own), out_dtype),
        grid_spec=pltpu.PrefetchScalarGridSpec(
            num_scalar_prefetch=3,
            grid=(owners, 2),
            in_specs=in_specs,
            out_specs=pl.BlockSpec((1, groups, span, slab_own), lambda x, m, *_: (x, 0, 0, m)),
            scratch_shapes=[
                pltpu.VMEM((2 * own.shape[0], width), jnp.bfloat16),
                pltpu.VMEM((slab_own, width), jnp.bfloat16),
            ],
        ),
        compiler_params=pltpu.CompilerParams(vmem_limit_bytes=40 * MIB),
        cost_estimate=pl.CostEstimate(
            flops=flops, bytes_accessed=2 * slab_own * owners * width * 2, transcendentals=0
        ),
    )(place, scale_num, mask, *operands)


def finish_kernel(rows, part_ref, out_ref, total):
    step = pl.program_id(0)
    here = jnp.sum(part_ref[...].astype(jnp.float32), axis=0)

    @pl.when(step == 0)
    def _():
        total[...] = here

    @pl.when(step != 0)
    def _():
        total[...] += here

    @pl.when(step == pl.num_programs(0) - 1)
    def _():
        slab_own = out_ref.shape[1]
        value = silu_times(total[:, :slab_own], total[:, slab_own:])
        split = value.reshape(CORES, -1, rows, slab_own)
        pieces = [split[core, x] for x in range(split.shape[1]) for core in range(CORES)]
        out_ref[...] = jnp.concatenate(pieces, axis=0).astype(out_ref.dtype)


def finish(parts, rows):
    sources, span, both = parts.shape
    block = min(sources, 16)
    return pl.pallas_call(
        functools.partial(finish_kernel, rows),
        out_shape=jax.ShapeDtypeStruct((span, both // 2), jnp.bfloat16),
        grid=(sources // block,),
        in_specs=[pl.BlockSpec((block, span, both), lambda i: (i, 0, 0))],
        out_specs=pl.BlockSpec((span, both // 2), lambda i: (0, 0)),
        scratch_shapes=[pltpu.VMEM((span, both), jnp.float32)],
        compiler_params=pltpu.CompilerParams(vmem_limit_bytes=32 * MIB),
        cost_estimate=pl.CostEstimate(
            flops=parts.size, bytes_accessed=2 * parts.size, transcendentals=span * both // 2
        ),
    )(parts)


def local_any(delta, drop_mask, scale_num, base, tokens, *, ckpts, groups):
    owners = ckpts // CORES
    both = ("ckpt", "tensor")
    same_core = [
        [(x * CORES + core) * groups + t for x in range(owners) for t in range(groups)]
        for core in range(CORES)
    ]
    swap = [(i, i ^ 1) for i in range(ckpts)]
    rows, width = tokens.shape
    width //= groups
    slab_own = base.shape[1]
    me = lax.axis_index("ckpt")
    row, core = me // CORES, me % CORES

    cut = tokens.reshape(rows, groups, width).transpose(1, 0, 2)
    send = jnp.broadcast_to(cut[None], (owners, groups, rows, width)).reshape(-1, rows, width)
    own = lax.all_to_all(send, both, 0, 0, axis_index_groups=same_core, tiled=True)
    own = own.reshape(owners * groups * rows, width)
    sib = lax.ppermute(own, "ckpt", swap)

    common = (own, sib, delta[0])
    place = jnp.stack([row, core, 1 - core]).astype(jnp.int32)
    theirs = partials(place, scale_num, drop_mask[0], *common, None, slab_own, groups, rows)
    arrived = lax.ppermute(theirs, "ckpt", swap)
    place = jnp.stack([row, core, core]).astype(jnp.int32)
    ours = partials(place, scale_num, drop_mask[0], *common, base, slab_own, groups, rows)
    chip = (ours + arrived.astype(jnp.float32)).astype(jnp.bfloat16)
    chip = chip.reshape(owners * groups, -1, 2 * slab_own)
    parts = lax.all_to_all(chip, both, 0, 0, axis_index_groups=same_core, tiled=True)
    return finish(parts, rows)


def solution(mesh):
    ckpts, groups = mesh.shape["ckpt"], mesh.shape["tensor"]
    if ckpts == 2 * CORES:
        local = functools.partial(local_pair, groups=groups)
    else:
        local = functools.partial(local_any, ckpts=ckpts, groups=groups)
    in_specs = (
        P("ckpt", None, None, "tensor"),
        P("ckpt", None, None, "tensor"),
        P("ckpt"),
        P(None, "ckpt", "tensor"),
        P(("tensor", "ckpt"), None),
    )
    out_specs = P("tensor", "ckpt")
    return jax.shard_map(local, mesh=mesh, in_specs=in_specs, out_specs=out_specs, check_vma=False)
```

```python
import functools

import jax
import jax.numpy as jnp
from jax import lax
from jax.experimental import pallas as pl
from jax.experimental.pallas import tpu as pltpu
from jax.sharding import PartitionSpec as P

BLOCK = 128
DEN = 16
CORES = 2
MIB = 1 << 20
VMEM = pl.BlockSpec(memory_space=pltpu.VMEM)
SMEM = pl.BlockSpec(memory_space=pltpu.SMEM)
HBM = pl.BlockSpec(memory_space=pltpu.HBM)


def dot_rows(tokens, weights):
    return lax.dot_general(
        tokens, weights, (((1,), (1,)), ((), ())), preferred_element_type=jnp.float32
    )


def silu_times(gate, up):
    return gate / (1 + jnp.exp(-gate)) * up


def gather_held(held, pieces):
    for i, piece in enumerate(pieces):
        span = piece.shape[0]
        held[i * span : (i + 1) * span] = piece[...]


def expand(mask, scale, factors):
    blocks, width = mask.shape[-1], factors.shape[1]
    column = lax.broadcasted_iota(jnp.int32, (blocks, width), 1) // BLOCK
    row = lax.broadcasted_iota(jnp.int32, (blocks, width), 0)
    spread = jnp.where(column == row, 1.0, 0.0).astype(jnp.float32)
    kept = jnp.where(mask.reshape(-1, blocks) != 0, scale, 0.0).astype(jnp.float32)
    rows = kept.shape[0]
    factors[:rows] = jnp.dot(kept, spread, preferred_element_type=jnp.float32)
    factors[rows:] = jnp.ones((factors.shape[0] - rows, width), jnp.float32)


def product(held, factors, weights, first):
    scaled = []
    for i in range(weights.shape[0] // BLOCK):
        factor = factors[pl.ds(first + i, 1), :].astype(weights.dtype)
        scaled.append(weights[i * BLOCK : (i + 1) * BLOCK] * factor)
    return dot_rows(held, jnp.concatenate(scaled, axis=0))


def chip_and_core():
    me = lax.axis_index("ckpt")
    return me >> 1, me & 1


def put(view, total, core):
    groups, rows = view.shape[0], view.shape[-2]
    split = total.reshape(-1, CORES, groups, rows, total.shape[-1])
    for x in range(split.shape[0]):
        for side in range(CORES):
            at = core if side == 0 else 1 - core
            for g in range(groups):
                here = (g, at) if len(view.shape) == 4 else (g, x, at)
                view[here] = split[x, side, g].astype(view.dtype)


class Rows:
    def __init__(self, source, kept, sems, owners, first=0):
        self.source, self.kept, self.sems, self.owners, self.first = source, kept, sems, owners, first

    def owner(self, part):
        owner = self.owners[0]
        return owner if len(self.owners) == 1 else jnp.where(part < 2, owner, self.owners[1])

    def copies(self, part):
        slab_own, chunks = self.kept.shape[1], self.sems.shape[1]
        span = slab_own // chunks
        at = self.first + part
        for h in range(chunks):
            rows = pl.ds(pl.multiple_of(self.owner(part) * slab_own + h * span, span), span)
            yield pltpu.make_async_copy(
                self.source.at[part % 2, rows, :],
                self.kept.at[at, pl.ds(h * span, span), :],
                self.sems.at[at, h],
            )

    def start(self):
        for part in range(2 * len(self.owners)):
            for copy in self.copies(part):
                copy.start()

    def wait(self, part):
        for copy in self.copies(part):
            copy.wait()


def first_factor(kept, factors, part, owner):
    strips = kept.shape[1] // BLOCK
    blocks = (factors.shape[0] - strips) // 2
    return part % 2 * blocks + owner * strips


def early_kernel(
    scale_num, mask_hbm, own, sib, delta, theirs, ours, kept, factors, held, mask, sems, mask_sem
):
    chip, core = chip_and_core()
    mask_copy = pltpu.make_async_copy(mask_hbm, mask, mask_sem)
    mask_copy.start()
    rows = Rows(delta, kept, sems, [(1 - chip) * CORES + at for at in (1 - core, core)])
    rows.start()
    gather_held(held, (own, sib))
    mask_copy.wait()
    expand(mask[...], scale_num[0].astype(jnp.float32) / DEN, factors)

    @pl.loop(0, 4)
    def _(part):
        rows.wait(part)
        first = first_factor(kept, factors, part, rows.owner(part))
        total = product(held[...], factors, kept.at[part], first)
        pl.when(part < 2)(lambda: put(theirs.at[part % 2], total, core))
        pl.when(part >= 2)(lambda: put(ours.at[part % 2], total, core))


def later_kernel(
    factors, own, sib, far_own, far_sib, kept, delta, theirs, ours, theirs_home, home, held, sems
):
    chip, core = chip_and_core()
    half = held.shape[0] // 2
    rows = Rows(delta, home, sems, [chip * CORES + 1 - core])
    rows.start()
    gather_held(held, (own, sib, far_own, far_sib))
    far = Rows(None, kept, None, [(1 - chip) * CORES + at for at in (1 - core, core)])

    @pl.loop(0, 4)
    def _(part):
        first = first_factor(kept, factors, part, far.owner(part))
        total = product(held[half:], factors, kept.at[part], first)
        pl.when(part < 2)(lambda: put(theirs.at[part % 2], total, core))
        pl.when(part >= 2)(lambda: put(ours.at[part % 2], total, core))

    @pl.loop(0, 2)
    def _(part):
        rows.wait(part)
        first = first_factor(home, factors, part, rows.owner(part))
        put(theirs_home.at[part], product(held[...], factors, home.at[part], first), core)


def home_kernel(factors, own, sib, far_own, far_sib, delta, base, ours, kept, held, total, sems):
    chip, core = chip_and_core()
    rows = Rows(delta, kept, sems, [chip * CORES + core])
    base_rows = Rows(base, kept, sems, [0], first=2)
    rows.start()
    base_rows.start()
    gather_held(held, (own, sib, far_own, far_sib))
    total[...] = jnp.zeros_like(total)
    ones = factors.shape[0] - kept.shape[1] // BLOCK

    @pl.loop(0, 4)
    def _(part):
        pl.when(part < 2)(lambda: rows.wait(part))
        pl.when(part >= 2)(lambda: base_rows.wait(part - 2))
        first = jnp.where(part < 2, first_factor(kept, factors, part, rows.owner(part)), ones)
        total[part % 2] += product(held[...], factors, kept.at[part], first)

    for m in range(2):
        put(ours.at[m], total[m], core)


def call(kernel, outs, scratch, in_specs, operands, flops, traffic):
    return pl.pallas_call(
        kernel,
        out_shape=outs,
        in_specs=in_specs,
        out_specs=[VMEM] * len(outs),
        scratch_shapes=scratch,
        compiler_params=pltpu.CompilerParams(vmem_limit_bytes=20 * MIB),
        cost_estimate=pl.CostEstimate(flops=flops // 8, bytes_accessed=traffic // 8, transcendentals=0),
    )(*operands)


def join_kernel(ours, arrived, out):
    out[...] = (ours[...] + arrived[...].astype(jnp.float32)).astype(out.dtype)


def join_home_kernel(ours, arrived, near, far, out):
    slab_own = ours.shape[-1]
    for m in range(2):
        for x, other in enumerate((near, far)):
            total = ours[m, :, x] + arrived[m, :, x].astype(jnp.float32)
            total = total + other[m].astype(jnp.float32)
            out[:, x, :, :, m * slab_own : (m + 1) * slab_own] = total.astype(out.dtype)


def last_kernel(parts, out, total):
    chip, _ = chip_and_core()
    rows = parts.shape[-2]
    slab_own = out.shape[1]
    for x in range(2):
        at = chip if x == 0 else 1 - chip
        for c in range(CORES):
            both = jnp.sum(parts[:, x, c].astype(jnp.float32), axis=0)
            value = silu_times(both[:, :slab_own], both[:, slab_own:])
            total[pl.ds(pl.multiple_of((at * CORES + c) * rows, rows), rows), :] = value
    out[...] = total[...].astype(out.dtype)


def local_pair(delta, drop_mask, scale_num, base, tokens, *, groups):
    rows, width = tokens.shape[0], tokens.shape[1] // groups
    slab_own = base.shape[1]
    f32, bf16 = jnp.float32, jnp.bfloat16
    in_hbm = lambda x: pltpu.with_memory_space_constraint(x, pltpu.HBM)
    mask, delta, base = in_hbm(drop_mask[0]), in_hbm(delta[0]), in_hbm(base)
    core_swap = functools.partial(lax.ppermute, axis_name="ckpt", perm=[(i, i ^ 1) for i in range(4)])
    chip_swap = functools.partial(lax.ppermute, axis_name="ckpt", perm=[(i, i ^ 2) for i in range(4)])

    cut = tokens.reshape(rows, groups, width).transpose(1, 0, 2)
    own = lax.all_to_all(cut, "tensor", 0, 0, tiled=True).reshape(groups * rows, width)
    far_own = chip_swap(own)
    sib = core_swap(own)

    half = groups * rows * CORES
    chunks = 2
    part = jax.ShapeDtypeStruct
    pair = (2, groups, CORES, rows, slab_own)
    four = (2, groups, 2, CORES, rows, slab_own)
    weights = (4, slab_own, width)
    size = 4 * slab_own * width
    blocks = mask.shape[0] * mask.shape[1] + slab_own // BLOCK
    theirs, ours, kept, factors = call(
        early_kernel,
        [part(pair, bf16), part(pair, f32), part(weights, bf16), part((blocks, width), f32)],
        [
            pltpu.VMEM((half, width), bf16),
            pltpu.VMEM(mask.shape, mask.dtype),
            pltpu.SemaphoreType.DMA((4, chunks)),
            pltpu.SemaphoreType.DMA(()),
        ],
        [SMEM, HBM, VMEM, VMEM, HBM],
        (scale_num, mask, own, sib, delta),
        2 * half * size,
        2 * size,
    )
    near = core_swap(theirs)
    far_own, theirs = lax.optimization_barrier((far_own, theirs))
    far_sib = core_swap(far_own)
    simple = lambda kernel, shape, *xs: pl.pallas_call(
        kernel,
        out_shape=part(shape, bf16),
        in_specs=[VMEM] * len(xs),
        out_specs=VMEM,
        compiler_params=pltpu.CompilerParams(vmem_limit_bytes=16 * MIB),
        cost_estimate=pl.CostEstimate(flops=xs[0].size, bytes_accessed=8 * xs[0].size, transcendentals=0),
    )(*xs)
    first, far_sib = lax.optimization_barrier((simple(join_kernel, pair, ours, near), far_sib))
    over_first = chip_swap(first)
    theirs, ours, theirs_home = call(
        later_kernel,
        [part(pair, bf16), part(pair, f32), part(four, bf16)],
        [
            pltpu.VMEM((2, slab_own, width), bf16),
            pltpu.VMEM((2 * half, width), bf16),
            pltpu.SemaphoreType.DMA((2, chunks)),
        ],
        [VMEM] * 6 + [HBM],
        (factors, own, sib, far_own, far_sib, kept, delta),
        4 * half * size,
        2 * size,
    )
    theirs, theirs_home, over_first = lax.optimization_barrier((theirs, theirs_home, over_first))
    second = simple(join_kernel, pair, ours, core_swap(theirs))
    near_home = core_swap(theirs_home)
    second, own = lax.optimization_barrier((second, own))
    over_second = chip_swap(second)
    (ours,) = call(
        home_kernel,
        [part(four, f32)],
        [
            pltpu.VMEM(weights, bf16),
            pltpu.VMEM((2 * half, width), bf16),
            pltpu.VMEM((2, 2 * half, slab_own), f32),
            pltpu.SemaphoreType.DMA((4, chunks)),
        ],
        [VMEM] * 5 + [HBM, HBM],
        (factors, own, sib, far_own, far_sib, delta, base),
        4 * half * size,
        2 * size,
    )
    whole = simple(
        join_home_kernel, (groups, 2, CORES, rows, 2 * slab_own), ours, near_home, over_second, over_first
    )
    parts = lax.all_to_all(whole, "tensor", 0, 0, tiled=True)
    return pl.pallas_call(
        last_kernel,
        out_shape=part((2 * CORES * rows, slab_own), bf16),
        in_specs=[VMEM],
        out_specs=VMEM,
        scratch_shapes=[pltpu.VMEM((2 * CORES * rows, slab_own), f32)],
        compiler_params=pltpu.CompilerParams(vmem_limit_bytes=16 * MIB),
    )(parts)


def masked_rows(mask_ref, delta_ref, kept, m, row_block):
    for i in range(kept.shape[0] // BLOCK):
        for j in range(kept.shape[1] // BLOCK):
            keep = mask_ref[m, row_block * (kept.shape[0] // BLOCK) + i, j] != 0
            here = (slice(i * BLOCK, (i + 1) * BLOCK), slice(j * BLOCK, (j + 1) * BLOCK))
            piece = delta_ref[0, here[0], here[1]]
            kept[here] = jnp.where(keep, piece, jnp.zeros_like(piece))


def partial_kernel(with_base, rows, place_ref, scale_ref, mask_ref, own_ref, sib_ref, delta_ref, *rest):
    if with_base:
        base_ref, out_ref, held, kept = rest
    else:
        out_ref, held, kept = rest
    row, core = place_ref[0], place_ref[1]
    target = place_ref[2]
    step, m = pl.program_id(0), pl.program_id(1)

    @pl.when((step == 0) & (m == 0))
    def _():
        half = own_ref.shape[0]
        held[:half] = own_ref[...]
        held[half:] = sib_ref[...]

    masked_rows(mask_ref, delta_ref, kept, m, step * CORES + target)
    scale = scale_ref[0].astype(jnp.float32) / DEN

    def store(total):
        groups = out_ref.shape[1]
        split = total.reshape(CORES, -1, groups, rows, total.shape[-1])
        span = split.shape[1] * rows
        for side, at in ((0, core), (1, 1 - core)):
            for g in range(groups):
                piece = split[side, :, g].reshape(span, -1).astype(out_ref.dtype)
                out_ref[0, g, pl.ds(pl.multiple_of(at * span, span), span), :] = piece

    product = scale * dot_rows(held[...], kept[...])
    if with_base:

        @pl.when(step == row)
        def _():
            store(product + dot_rows(held[...], base_ref[0]))

        @pl.when(step != row)
        def _():
            store(product)

    else:
        store(product)


def partials(place, scale_num, mask, own, sib, delta, base, slab_own, groups, rows):
    width = delta.shape[2]
    owners = delta.shape[1] // slab_own // CORES
    span = 2 * own.shape[0] // groups
    whole = lambda *_: (0, 0)
    in_specs = [
        pl.BlockSpec(own.shape, whole),
        pl.BlockSpec(sib.shape, whole),
        pl.BlockSpec((1, slab_own, width), lambda x, m, place, *_: (m, x * CORES + place[2], 0)),
    ]
    operands = [own, sib, delta]
    if base is not None:
        in_specs.append(pl.BlockSpec((1, slab_own, width), lambda x, m, *_: (m, 0, 0)))
        operands.append(base)
    out_dtype = jnp.bfloat16 if base is None else jnp.float32
    flops = 2 * 2 * own.shape[0] * width * 2 * slab_own * owners
    return pl.pallas_call(
        functools.partial(partial_kernel, base is not None, rows),
        out_shape=jax.ShapeDtypeStruct((owners, groups, span, 2 * slab_own), out_dtype),
        grid_spec=pltpu.PrefetchScalarGridSpec(
            num_scalar_prefetch=3,
            grid=(owners, 2),
            in_specs=in_specs,
            out_specs=pl.BlockSpec((1, groups, span, slab_own), lambda x, m, *_: (x, 0, 0, m)),
            scratch_shapes=[
                pltpu.VMEM((2 * own.shape[0], width), jnp.bfloat16),
                pltpu.VMEM((slab_own, width), jnp.bfloat16),
            ],
        ),
        compiler_params=pltpu.CompilerParams(vmem_limit_bytes=40 * MIB),
        cost_estimate=pl.CostEstimate(
            flops=flops, bytes_accessed=2 * slab_own * owners * width * 2, transcendentals=0
        ),
    )(place, scale_num, mask, *operands)


def finish_kernel(rows, part_ref, out_ref, total):
    step = pl.program_id(0)
    here = jnp.sum(part_ref[...].astype(jnp.float32), axis=0)

    @pl.when(step == 0)
    def _():
        total[...] = here

    @pl.when(step != 0)
    def _():
        total[...] += here

    @pl.when(step == pl.num_programs(0) - 1)
    def _():
        slab_own = out_ref.shape[1]
        value = silu_times(total[:, :slab_own], total[:, slab_own:])
        split = value.reshape(CORES, -1, rows, slab_own)
        pieces = [split[core, x] for x in range(split.shape[1]) for core in range(CORES)]
        out_ref[...] = jnp.concatenate(pieces, axis=0).astype(out_ref.dtype)


def finish(parts, rows):
    sources, span, both = parts.shape
    block = min(sources, 16)
    return pl.pallas_call(
        functools.partial(finish_kernel, rows),
        out_shape=jax.ShapeDtypeStruct((span, both // 2), jnp.bfloat16),
        grid=(sources // block,),
        in_specs=[pl.BlockSpec((block, span, both), lambda i: (i, 0, 0))],
        out_specs=pl.BlockSpec((span, both // 2), lambda i: (0, 0)),
        scratch_shapes=[pltpu.VMEM((span, both), jnp.float32)],
        compiler_params=pltpu.CompilerParams(vmem_limit_bytes=32 * MIB),
        cost_estimate=pl.CostEstimate(
            flops=parts.size, bytes_accessed=2 * parts.size, transcendentals=span * both // 2
        ),
    )(parts)


def local_any(delta, drop_mask, scale_num, base, tokens, *, ckpts, groups):
    owners = ckpts // CORES
    both = ("ckpt", "tensor")
    same_core = [
        [(x * CORES + core) * groups + t for x in range(owners) for t in range(groups)]
        for core in range(CORES)
    ]
    swap = [(i, i ^ 1) for i in range(ckpts)]
    rows, width = tokens.shape
    width //= groups
    slab_own = base.shape[1]
    me = lax.axis_index("ckpt")
    row, core = me // CORES, me % CORES

    cut = tokens.reshape(rows, groups, width).transpose(1, 0, 2)
    send = jnp.broadcast_to(cut[None], (owners, groups, rows, width)).reshape(-1, rows, width)
    own = lax.all_to_all(send, both, 0, 0, axis_index_groups=same_core, tiled=True)
    own = own.reshape(owners * groups * rows, width)
    sib = lax.ppermute(own, "ckpt", swap)

    common = (own, sib, delta[0])
    place = jnp.stack([row, core, 1 - core]).astype(jnp.int32)
    theirs = partials(place, scale_num, drop_mask[0], *common, None, slab_own, groups, rows)
    arrived = lax.ppermute(theirs, "ckpt", swap)
    place = jnp.stack([row, core, core]).astype(jnp.int32)
    ours = partials(place, scale_num, drop_mask[0], *common, base, slab_own, groups, rows)
    chip = (ours + arrived.astype(jnp.float32)).astype(jnp.bfloat16)
    chip = chip.reshape(owners * groups, -1, 2 * slab_own)
    parts = lax.all_to_all(chip, both, 0, 0, axis_index_groups=same_core, tiled=True)
    return finish(parts, rows)


def solution(mesh):
    ckpts, groups = mesh.shape["ckpt"], mesh.shape["tensor"]
    if ckpts == 2 * CORES:
        local = functools.partial(local_pair, groups=groups)
    else:
        local = functools.partial(local_any, ckpts=ckpts, groups=groups)
    in_specs = (
        P("ckpt", None, None, "tensor"),
        P("ckpt", None, None, "tensor"),
        P("ckpt"),
        P(None, "ckpt", "tensor"),
        P(("tensor", "ckpt"), None),
    )
    out_specs = P("tensor", "ckpt")
    return jax.shard_map(local, mesh=mesh, in_specs=in_specs, out_specs=out_specs, check_vma=False)
```

```python
import functools

import jax
import jax.numpy as jnp
from jax import lax
from jax.experimental import pallas as pl
from jax.experimental.pallas import tpu as pltpu
from jax.sharding import PartitionSpec as P

BLOCK = 128
DEN = 16
CORES = 2
MIB = 1 << 20
VMEM = pl.BlockSpec(memory_space=pltpu.VMEM)
SMEM = pl.BlockSpec(memory_space=pltpu.SMEM)
HBM = pl.BlockSpec(memory_space=pltpu.HBM)


def dot_rows(tokens, weights):
    return lax.dot_general(
        tokens, weights, (((1,), (1,)), ((), ())), preferred_element_type=jnp.float32
    )


def silu_times(gate, up):
    return gate / (1 + jnp.exp(-gate)) * up


def gather_held(held, pieces):
    for i, piece in enumerate(pieces):
        span = piece.shape[0]
        held[i * span : (i + 1) * span] = piece[...]


def expand(mask, scale, factors):
    blocks, width = mask.shape[-1], factors.shape[1]
    column = lax.broadcasted_iota(jnp.int32, (blocks, width), 1) // BLOCK
    row = lax.broadcasted_iota(jnp.int32, (blocks, width), 0)
    spread = jnp.where(column == row, 1.0, 0.0).astype(jnp.float32)
    kept = jnp.where(mask.reshape(-1, blocks) != 0, scale, 0.0).astype(jnp.float32)
    rows = kept.shape[0]
    factors[:rows] = jnp.dot(kept, spread, preferred_element_type=jnp.float32)
    factors[rows:] = jnp.ones((factors.shape[0] - rows, width), jnp.float32)


def product(held, factors, weights, first):
    scaled = []
    for i in range(weights.shape[0] // BLOCK):
        factor = factors[pl.ds(first + i, 1), :].astype(weights.dtype)
        scaled.append(weights[i * BLOCK : (i + 1) * BLOCK] * factor)
    return dot_rows(held, jnp.concatenate(scaled, axis=0))


def chip_and_core():
    me = lax.axis_index("ckpt")
    return me >> 1, me & 1


def put(view, total, core):
    groups, rows = view.shape[0], view.shape[-2]
    split = total.reshape(-1, CORES, groups, rows, total.shape[-1])
    for x in range(split.shape[0]):
        for side in range(CORES):
            at = core if side == 0 else 1 - core
            for g in range(groups):
                here = (g, at) if len(view.shape) == 4 else (g, x, at)
                view[here] = split[x, side, g].astype(view.dtype)


class Rows:
    def __init__(self, source, kept, sems, owners, first=0):
        self.source, self.kept, self.sems, self.owners, self.first = source, kept, sems, owners, first

    def owner(self, part):
        owner = self.owners[0]
        return owner if len(self.owners) == 1 else jnp.where(part < 2, owner, self.owners[1])

    def copies(self, part):
        slab_own, chunks = self.kept.shape[1], self.sems.shape[1]
        span = slab_own // chunks
        at = self.first + part
        for h in range(chunks):
            rows = pl.ds(pl.multiple_of(self.owner(part) * slab_own + h * span, span), span)
            yield pltpu.make_async_copy(
                self.source.at[part % 2, rows, :],
                self.kept.at[at, pl.ds(h * span, span), :],
                self.sems.at[at, h],
            )

    def start(self):
        for part in range(2 * len(self.owners)):
            for copy in self.copies(part):
                copy.start()

    def wait(self, part):
        for copy in self.copies(part):
            copy.wait()


def first_factor(kept, factors, part, owner):
    strips = kept.shape[1] // BLOCK
    blocks = (factors.shape[0] - strips) // 2
    return part % 2 * blocks + owner * strips


def early_kernel(
    scale_num, mask_hbm, own, sib, delta, theirs, kept, factors, held, mask, sems, mask_sem
):
    chip, core = chip_and_core()
    mask_copy = pltpu.make_async_copy(mask_hbm, mask, mask_sem)
    mask_copy.start()
    rows = Rows(delta, kept, sems, [(1 - chip) * CORES + at for at in (1 - core, core)])
    rows.start()
    gather_held(held, (own, sib))
    mask_copy.wait()
    expand(mask[...], scale_num[0].astype(jnp.float32) / DEN, factors)

    @pl.loop(0, 2)
    def _(part):
        rows.wait(part)
        first = first_factor(kept, factors, part, rows.owner(part))
        put(theirs.at[part], product(held[...], factors, kept.at[part], first), core)

    for part in (2, 3):
        rows.wait(part)


def early_rest_kernel(factors, own, sib, kept, ours, held):
    chip, core = chip_and_core()
    gather_held(held, (own, sib))

    @pl.loop(0, 2)
    def _(part):
        first = first_factor(kept, factors, part, (1 - chip) * CORES + core)
        put(ours.at[part], product(held[...], factors, kept.at[2 + part], first), core)


def later_kernel(
    factors, own, sib, far_own, far_sib, kept, delta, theirs, ours, theirs_home, home, held, sems
):
    chip, core = chip_and_core()
    half = held.shape[0] // 2
    rows = Rows(delta, home, sems, [chip * CORES + 1 - core])
    rows.start()
    gather_held(held, (own, sib, far_own, far_sib))
    far = Rows(None, kept, None, [(1 - chip) * CORES + at for at in (1 - core, core)])

    @pl.loop(0, 4)
    def _(part):
        first = first_factor(kept, factors, part, far.owner(part))
        total = product(held[half:], factors, kept.at[part], first)
        pl.when(part < 2)(lambda: put(theirs.at[part % 2], total, core))
        pl.when(part >= 2)(lambda: put(ours.at[part % 2], total, core))

    @pl.loop(0, 2)
    def _(part):
        rows.wait(part)
        first = first_factor(home, factors, part, rows.owner(part))
        put(theirs_home.at[part], product(held[...], factors, home.at[part], first), core)


def home_kernel(factors, own, sib, far_own, far_sib, delta, base, ours, kept, held, total, sems):
    chip, core = chip_and_core()
    rows = Rows(delta, kept, sems, [chip * CORES + core])
    base_rows = Rows(base, kept, sems, [0], first=2)
    rows.start()
    base_rows.start()
    gather_held(held, (own, sib, far_own, far_sib))
    total[...] = jnp.zeros_like(total)
    ones = factors.shape[0] - kept.shape[1] // BLOCK

    @pl.loop(0, 4)
    def _(part):
        pl.when(part < 2)(lambda: rows.wait(part))
        pl.when(part >= 2)(lambda: base_rows.wait(part - 2))
        first = jnp.where(part < 2, first_factor(kept, factors, part, rows.owner(part)), ones)
        total[part % 2] += product(held[...], factors, kept.at[part], first)

    for m in range(2):
        put(ours.at[m], total[m], core)


def call(kernel, outs, scratch, in_specs, operands, flops, traffic):
    return pl.pallas_call(
        kernel,
        out_shape=outs,
        in_specs=in_specs,
        out_specs=[VMEM] * len(outs),
        scratch_shapes=scratch,
        compiler_params=pltpu.CompilerParams(vmem_limit_bytes=20 * MIB),
        cost_estimate=pl.CostEstimate(flops=flops // 8, bytes_accessed=traffic // 8, transcendentals=0),
    )(*operands)


def meet_kernel(arrived, out):
    first = (0,) * (len(arrived.shape) - 2)
    out[...] = arrived[first + (slice(0, out.shape[0]), slice(0, out.shape[1]))]


def join_kernel(ours, arrived, *rest):
    out = rest[-1]
    out[...] = (ours[...] + arrived[...].astype(jnp.float32)).astype(out.dtype)


def join_home_kernel(ours, arrived, near, far, out):
    slab_own = ours.shape[-1]
    for m in range(2):
        for x, other in enumerate((near, far)):
            total = ours[m, :, x] + arrived[m, :, x].astype(jnp.float32)
            total = total + other[m].astype(jnp.float32)
            out[:, x, :, :, m * slab_own : (m + 1) * slab_own] = total.astype(out.dtype)


def last_kernel(parts, out, total):
    chip, _ = chip_and_core()
    rows = parts.shape[-2]
    slab_own = out.shape[1]
    for x in range(2):
        at = chip if x == 0 else 1 - chip
        for c in range(CORES):
            both = jnp.sum(parts[:, x, c].astype(jnp.float32), axis=0)
            value = silu_times(both[:, :slab_own], both[:, slab_own:])
            total[pl.ds(pl.multiple_of((at * CORES + c) * rows, rows), rows), :] = value
    out[...] = total[...].astype(out.dtype)


def local_pair(delta, drop_mask, scale_num, base, tokens, *, groups):
    rows, width = tokens.shape[0], tokens.shape[1] // groups
    slab_own = base.shape[1]
    f32, bf16 = jnp.float32, jnp.bfloat16
    in_hbm = lambda x: pltpu.with_memory_space_constraint(x, pltpu.HBM)
    mask, delta, base = in_hbm(drop_mask[0]), in_hbm(delta[0]), in_hbm(base)
    core_swap = functools.partial(lax.ppermute, axis_name="ckpt", perm=[(i, i ^ 1) for i in range(4)])
    chip_swap = functools.partial(lax.ppermute, axis_name="ckpt", perm=[(i, i ^ 2) for i in range(4)])

    cut = tokens.reshape(rows, groups, width).transpose(1, 0, 2)
    own = lax.all_to_all(cut, "tensor", 0, 0, tiled=True).reshape(groups * rows, width)
    far_own = chip_swap(own)
    sib = core_swap(own)

    half = groups * rows * CORES
    chunks = 2
    part = jax.ShapeDtypeStruct
    pair = (2, groups, CORES, rows, slab_own)
    four = (2, groups, 2, CORES, rows, slab_own)
    weights = (4, slab_own, width)
    size = 4 * slab_own * width
    blocks = mask.shape[0] * mask.shape[1] + slab_own // BLOCK
    theirs, kept, factors = call(
        early_kernel,
        [part(pair, bf16), part(weights, bf16), part((blocks, width), f32)],
        [
            pltpu.VMEM((half, width), bf16),
            pltpu.VMEM(mask.shape, mask.dtype),
            pltpu.SemaphoreType.DMA((4, chunks)),
            pltpu.SemaphoreType.DMA(()),
        ],
        [SMEM, HBM, VMEM, VMEM, HBM],
        (scale_num, mask, own, sib, delta),
        half * size,
        2 * size,
    )
    near = core_swap(theirs)
    (ours,) = call(
        early_rest_kernel,
        [part(pair, f32)],
        [pltpu.VMEM((half, width), bf16)],
        [VMEM] * 4,
        (factors, own, sib, kept),
        8,
        8,
    )
    simple = lambda kernel, shape, *xs: pl.pallas_call(
        kernel,
        out_shape=part(shape, bf16),
        in_specs=[VMEM] * len(xs),
        out_specs=VMEM,
        compiler_params=pltpu.CompilerParams(vmem_limit_bytes=16 * MIB),
        cost_estimate=pl.CostEstimate(flops=xs[0].size, bytes_accessed=8 * xs[0].size, transcendentals=0),
    )(*xs)
    far_own, ours = lax.optimization_barrier((far_own, ours))
    met = simple(meet_kernel, (rows, BLOCK), far_own)
    over_first = chip_swap(simple(join_kernel, pair, ours, near, met))
    far_sib = core_swap(far_own)
    theirs, ours, theirs_home = call(
        later_kernel,
        [part(pair, bf16), part(pair, f32), part(four, bf16)],
        [
            pltpu.VMEM((2, slab_own, width), bf16),
            pltpu.VMEM((2 * half, width), bf16),
            pltpu.SemaphoreType.DMA((2, chunks)),
        ],
        [VMEM] * 6 + [HBM],
        (factors, own, sib, far_own, far_sib, kept, delta),
        4 * half * size,
        2 * size,
    )
    met = simple(meet_kernel, (rows, BLOCK), over_first)
    second = simple(join_kernel, pair, ours, core_swap(theirs), met)
    near_home = core_swap(theirs_home)
    second, own = lax.optimization_barrier((second, own))
    over_second = chip_swap(second)
    (ours,) = call(
        home_kernel,
        [part(four, f32)],
        [
            pltpu.VMEM(weights, bf16),
            pltpu.VMEM((2 * half, width), bf16),
            pltpu.VMEM((2, 2 * half, slab_own), f32),
            pltpu.SemaphoreType.DMA((4, chunks)),
        ],
        [VMEM] * 5 + [HBM, HBM],
        (factors, own, sib, far_own, far_sib, delta, base),
        4 * half * size,
        2 * size,
    )
    whole = simple(
        join_home_kernel, (groups, 2, CORES, rows, 2 * slab_own), ours, near_home, over_second, over_first
    )
    parts = lax.all_to_all(whole, "tensor", 0, 0, tiled=True)
    return pl.pallas_call(
        last_kernel,
        out_shape=part((2 * CORES * rows, slab_own), bf16),
        in_specs=[VMEM],
        out_specs=VMEM,
        scratch_shapes=[pltpu.VMEM((2 * CORES * rows, slab_own), f32)],
        compiler_params=pltpu.CompilerParams(vmem_limit_bytes=16 * MIB),
    )(parts)


def masked_rows(mask_ref, delta_ref, kept, m, row_block):
    for i in range(kept.shape[0] // BLOCK):
        for j in range(kept.shape[1] // BLOCK):
            keep = mask_ref[m, row_block * (kept.shape[0] // BLOCK) + i, j] != 0
            here = (slice(i * BLOCK, (i + 1) * BLOCK), slice(j * BLOCK, (j + 1) * BLOCK))
            piece = delta_ref[0, here[0], here[1]]
            kept[here] = jnp.where(keep, piece, jnp.zeros_like(piece))


def partial_kernel(with_base, rows, place_ref, scale_ref, mask_ref, own_ref, sib_ref, delta_ref, *rest):
    if with_base:
        base_ref, out_ref, held, kept = rest
    else:
        out_ref, held, kept = rest
    row, core = place_ref[0], place_ref[1]
    target = place_ref[2]
    step, m = pl.program_id(0), pl.program_id(1)

    @pl.when((step == 0) & (m == 0))
    def _():
        half = own_ref.shape[0]
        held[:half] = own_ref[...]
        held[half:] = sib_ref[...]

    masked_rows(mask_ref, delta_ref, kept, m, step * CORES + target)
    scale = scale_ref[0].astype(jnp.float32) / DEN

    def store(total):
        groups = out_ref.shape[1]
        split = total.reshape(CORES, -1, groups, rows, total.shape[-1])
        span = split.shape[1] * rows
        for side, at in ((0, core), (1, 1 - core)):
            for g in range(groups):
                piece = split[side, :, g].reshape(span, -1).astype(out_ref.dtype)
                out_ref[0, g, pl.ds(pl.multiple_of(at * span, span), span), :] = piece

    product = scale * dot_rows(held[...], kept[...])
    if with_base:

        @pl.when(step == row)
        def _():
            store(product + dot_rows(held[...], base_ref[0]))

        @pl.when(step != row)
        def _():
            store(product)

    else:
        store(product)


def partials(place, scale_num, mask, own, sib, delta, base, slab_own, groups, rows):
    width = delta.shape[2]
    owners = delta.shape[1] // slab_own // CORES
    span = 2 * own.shape[0] // groups
    whole = lambda *_: (0, 0)
    in_specs = [
        pl.BlockSpec(own.shape, whole),
        pl.BlockSpec(sib.shape, whole),
        pl.BlockSpec((1, slab_own, width), lambda x, m, place, *_: (m, x * CORES + place[2], 0)),
    ]
    operands = [own, sib, delta]
    if base is not None:
        in_specs.append(pl.BlockSpec((1, slab_own, width), lambda x, m, *_: (m, 0, 0)))
        operands.append(base)
    out_dtype = jnp.bfloat16 if base is None else jnp.float32
    flops = 2 * 2 * own.shape[0] * width * 2 * slab_own * owners
    return pl.pallas_call(
        functools.partial(partial_kernel, base is not None, rows),
        out_shape=jax.ShapeDtypeStruct((owners, groups, span, 2 * slab_own), out_dtype),
        grid_spec=pltpu.PrefetchScalarGridSpec(
            num_scalar_prefetch=3,
            grid=(owners, 2),
            in_specs=in_specs,
            out_specs=pl.BlockSpec((1, groups, span, slab_own), lambda x, m, *_: (x, 0, 0, m)),
            scratch_shapes=[
                pltpu.VMEM((2 * own.shape[0], width), jnp.bfloat16),
                pltpu.VMEM((slab_own, width), jnp.bfloat16),
            ],
        ),
        compiler_params=pltpu.CompilerParams(vmem_limit_bytes=40 * MIB),
        cost_estimate=pl.CostEstimate(
            flops=flops, bytes_accessed=2 * slab_own * owners * width * 2, transcendentals=0
        ),
    )(place, scale_num, mask, *operands)


def finish_kernel(rows, part_ref, out_ref, total):
    step = pl.program_id(0)
    here = jnp.sum(part_ref[...].astype(jnp.float32), axis=0)

    @pl.when(step == 0)
    def _():
        total[...] = here

    @pl.when(step != 0)
    def _():
        total[...] += here

    @pl.when(step == pl.num_programs(0) - 1)
    def _():
        slab_own = out_ref.shape[1]
        value = silu_times(total[:, :slab_own], total[:, slab_own:])
        split = value.reshape(CORES, -1, rows, slab_own)
        pieces = [split[core, x] for x in range(split.shape[1]) for core in range(CORES)]
        out_ref[...] = jnp.concatenate(pieces, axis=0).astype(out_ref.dtype)


def finish(parts, rows):
    sources, span, both = parts.shape
    block = min(sources, 16)
    return pl.pallas_call(
        functools.partial(finish_kernel, rows),
        out_shape=jax.ShapeDtypeStruct((span, both // 2), jnp.bfloat16),
        grid=(sources // block,),
        in_specs=[pl.BlockSpec((block, span, both), lambda i: (i, 0, 0))],
        out_specs=pl.BlockSpec((span, both // 2), lambda i: (0, 0)),
        scratch_shapes=[pltpu.VMEM((span, both), jnp.float32)],
        compiler_params=pltpu.CompilerParams(vmem_limit_bytes=32 * MIB),
        cost_estimate=pl.CostEstimate(
            flops=parts.size, bytes_accessed=2 * parts.size, transcendentals=span * both // 2
        ),
    )(parts)


def local_any(delta, drop_mask, scale_num, base, tokens, *, ckpts, groups):
    owners = ckpts // CORES
    both = ("ckpt", "tensor")
    same_core = [
        [(x * CORES + core) * groups + t for x in range(owners) for t in range(groups)]
        for core in range(CORES)
    ]
    swap = [(i, i ^ 1) for i in range(ckpts)]
    rows, width = tokens.shape
    width //= groups
    slab_own = base.shape[1]
    me = lax.axis_index("ckpt")
    row, core = me // CORES, me % CORES

    cut = tokens.reshape(rows, groups, width).transpose(1, 0, 2)
    send = jnp.broadcast_to(cut[None], (owners, groups, rows, width)).reshape(-1, rows, width)
    own = lax.all_to_all(send, both, 0, 0, axis_index_groups=same_core, tiled=True)
    own = own.reshape(owners * groups * rows, width)
    sib = lax.ppermute(own, "ckpt", swap)

    common = (own, sib, delta[0])
    place = jnp.stack([row, core, 1 - core]).astype(jnp.int32)
    theirs = partials(place, scale_num, drop_mask[0], *common, None, slab_own, groups, rows)
    arrived = lax.ppermute(theirs, "ckpt", swap)
    place = jnp.stack([row, core, core]).astype(jnp.int32)
    ours = partials(place, scale_num, drop_mask[0], *common, base, slab_own, groups, rows)
    chip = (ours + arrived.astype(jnp.float32)).astype(jnp.bfloat16)
    chip = chip.reshape(owners * groups, -1, 2 * slab_own)
    parts = lax.all_to_all(chip, both, 0, 0, axis_index_groups=same_core, tiled=True)
    return finish(parts, rows)


def solution(mesh):
    ckpts, groups = mesh.shape["ckpt"], mesh.shape["tensor"]
    if ckpts == 2 * CORES:
        local = functools.partial(local_pair, groups=groups)
    else:
        local = functools.partial(local_any, ckpts=ckpts, groups=groups)
    in_specs = (
        P("ckpt", None, None, "tensor"),
        P("ckpt", None, None, "tensor"),
        P("ckpt"),
        P(None, "ckpt", "tensor"),
        P(("tensor", "ckpt"), None),
    )
    out_specs = P("tensor", "ckpt")
    return jax.shard_map(local, mesh=mesh, in_specs=in_specs, out_specs=out_specs, check_vma=False)
```

```python
import functools

import jax
import jax.numpy as jnp
from jax import lax
from jax.experimental import pallas as pl
from jax.experimental.pallas import tpu as pltpu
from jax.sharding import PartitionSpec as P

BLOCK = 128
DEN = 16
CORES = 2
MIB = 1 << 20
VMEM = pl.BlockSpec(memory_space=pltpu.VMEM)
SMEM = pl.BlockSpec(memory_space=pltpu.SMEM)
HBM = pl.BlockSpec(memory_space=pltpu.HBM)


def dot_rows(tokens, weights):
    return lax.dot_general(
        tokens, weights, (((1,), (1,)), ((), ())), preferred_element_type=jnp.float32
    )


def silu_times(gate, up):
    return gate / (1 + jnp.exp(-gate)) * up


def gather_held(held, pieces):
    for i, piece in enumerate(pieces):
        span = piece.shape[0]
        held[i * span : (i + 1) * span] = piece[...]


def expand(mask, scale, factors):
    blocks, width = mask.shape[-1], factors.shape[1]
    column = lax.broadcasted_iota(jnp.int32, (blocks, width), 1) // BLOCK
    row = lax.broadcasted_iota(jnp.int32, (blocks, width), 0)
    spread = jnp.where(column == row, 1.0, 0.0).astype(jnp.float32)
    kept = jnp.where(mask.reshape(-1, blocks) != 0, scale, 0.0).astype(jnp.float32)
    rows = kept.shape[0]
    factors[:rows] = jnp.dot(kept, spread, preferred_element_type=jnp.float32)
    factors[rows:] = jnp.ones((factors.shape[0] - rows, width), jnp.float32)


def product(held, factors, weights, first):
    scaled = []
    for i in range(weights.shape[0] // BLOCK):
        factor = factors[pl.ds(first + i, 1), :].astype(weights.dtype)
        scaled.append(weights[i * BLOCK : (i + 1) * BLOCK] * factor)
    return dot_rows(held, jnp.concatenate(scaled, axis=0))


def chip_and_core():
    me = lax.axis_index("ckpt")
    return me >> 1, me & 1


def put(view, total, core):
    groups, rows = view.shape[0], view.shape[-2]
    split = total.reshape(-1, CORES, groups, rows, total.shape[-1])
    for x in range(split.shape[0]):
        for side in range(CORES):
            at = core if side == 0 else 1 - core
            for g in range(groups):
                here = (g, at) if len(view.shape) == 4 else (g, x, at)
                view[here] = split[x, side, g].astype(view.dtype)


class Rows:
    def __init__(self, source, kept, sems, owners, first=0):
        self.source, self.kept, self.sems, self.owners, self.first = source, kept, sems, owners, first

    def owner(self, part):
        owner = self.owners[0]
        return owner if len(self.owners) == 1 else jnp.where(part < 2, owner, self.owners[1])

    def copies(self, part):
        slab_own, chunks = self.kept.shape[1], self.sems.shape[1]
        span = slab_own // chunks
        at = self.first + part
        for h in range(chunks):
            rows = pl.ds(pl.multiple_of(self.owner(part) * slab_own + h * span, span), span)
            yield pltpu.make_async_copy(
                self.source.at[part % 2, rows, :],
                self.kept.at[at, pl.ds(h * span, span), :],
                self.sems.at[at, h],
            )

    def start(self):
        for part in range(2 * len(self.owners)):
            for copy in self.copies(part):
                copy.start()

    def wait(self, part):
        for copy in self.copies(part):
            copy.wait()


def first_factor(kept, factors, part, owner):
    strips = kept.shape[1] // BLOCK
    blocks = (factors.shape[0] - strips) // 2
    return part % 2 * blocks + owner * strips


def early_kernel(
    scale_num, mask_hbm, own, sib, delta, gate, up, kept, factors, held, mask, sems, mask_sem
):
    chip, core = chip_and_core()
    mask_copy = pltpu.make_async_copy(mask_hbm, mask, mask_sem)
    mask_copy.start()
    rows = Rows(delta, kept, sems, [(1 - chip) * CORES + at for at in (1 - core, core)])
    rows.start()
    gather_held(held, (own, sib))
    mask_copy.wait()
    expand(mask[...], scale_num[0].astype(jnp.float32) / DEN, factors)

    @pl.loop(0, 2)
    def _(part):
        rows.wait(part)
        first = first_factor(kept, factors, part, rows.owner(part))
        total = product(held[...], factors, kept.at[part], first)
        pl.when(part == 0)(lambda: put(gate, total, core))
        pl.when(part == 1)(lambda: put(up, total, core))

    for part in (2, 3):
        rows.wait(part)


def early_rest_kernel(factors, own, sib, kept, ours, held):
    chip, core = chip_and_core()
    gather_held(held, (own, sib))

    @pl.loop(0, 2)
    def _(part):
        first = first_factor(kept, factors, part, (1 - chip) * CORES + core)
        put(ours.at[part], product(held[...], factors, kept.at[2 + part], first), core)


def later_kernel(factors, far_own, far_sib, kept, after, theirs, ours, held):
    chip, core = chip_and_core()
    gather_held(held, (far_own, far_sib))
    far = Rows(None, kept, None, [(1 - chip) * CORES + at for at in (1 - core, core)])

    @pl.loop(0, 4)
    def _(part):
        first = first_factor(kept, factors, part, far.owner(part))
        total = product(held[...], factors, kept.at[part], first)
        pl.when(part < 2)(lambda: put(theirs.at[part % 2], total, core))
        pl.when(part >= 2)(lambda: put(ours.at[part % 2], total, core))


def home_sib_kernel(factors, own, sib, far_own, far_sib, delta, theirs, home, held, sems):
    chip, core = chip_and_core()
    rows = Rows(delta, home, sems, [chip * CORES + 1 - core])
    rows.start()
    gather_held(held, (own, sib, far_own, far_sib))

    @pl.loop(0, 2)
    def _(part):
        rows.wait(part)
        first = first_factor(home, factors, part, rows.owner(part))
        put(theirs.at[part], product(held[...], factors, home.at[part], first), core)


def home_kernel(factors, own, sib, far_own, far_sib, delta, base, ours, kept, held, total, sems):
    chip, core = chip_and_core()
    rows = Rows(delta, kept, sems, [chip * CORES + core])
    base_rows = Rows(base, kept, sems, [0], first=2)
    rows.start()
    base_rows.start()
    gather_held(held, (own, sib, far_own, far_sib))
    total[...] = jnp.zeros_like(total)
    ones = factors.shape[0] - kept.shape[1] // BLOCK

    @pl.loop(0, 4)
    def _(part):
        pl.when(part < 2)(lambda: rows.wait(part))
        pl.when(part >= 2)(lambda: base_rows.wait(part - 2))
        first = jnp.where(part < 2, first_factor(kept, factors, part, rows.owner(part)), ones)
        total[part % 2] += product(held[...], factors, kept.at[part], first)

    for m in range(2):
        put(ours.at[m], total[m], core)


def call(kernel, outs, scratch, in_specs, operands, flops, traffic):
    return pl.pallas_call(
        kernel,
        out_shape=outs,
        in_specs=in_specs,
        out_specs=[VMEM] * len(outs),
        scratch_shapes=scratch,
        compiler_params=pltpu.CompilerParams(vmem_limit_bytes=20 * MIB),
        cost_estimate=pl.CostEstimate(flops=flops // 8, bytes_accessed=traffic // 8, transcendentals=0),
    )(*operands)


def meet_kernel(arrived, out):
    first = (0,) * (len(arrived.shape) - 2)
    out[...] = arrived[first + (slice(0, out.shape[0]), slice(0, out.shape[1]))]


def join_halves_kernel(ours, gate, up, out):
    for m, arrived in enumerate((gate, up)):
        out[m] = (ours[m] + arrived[...].astype(jnp.float32)).astype(out.dtype)


def join_kernel(ours, arrived, *rest):
    out = rest[-1]
    out[...] = (ours[...] + arrived[...].astype(jnp.float32)).astype(out.dtype)


def join_home_kernel(ours, arrived, near, far, out):
    slab_own = ours.shape[-1]
    for m in range(2):
        for x, other in enumerate((near, far)):
            total = ours[m, :, x] + arrived[m, :, x].astype(jnp.float32)
            total = total + other[m].astype(jnp.float32)
            out[:, x, :, :, m * slab_own : (m + 1) * slab_own] = total.astype(out.dtype)


def last_kernel(parts, out, total):
    chip, _ = chip_and_core()
    rows = parts.shape[-2]
    slab_own = out.shape[1]
    for x in range(2):
        at = chip if x == 0 else 1 - chip
        for c in range(CORES):
            both = jnp.sum(parts[:, x, c].astype(jnp.float32), axis=0)
            value = silu_times(both[:, :slab_own], both[:, slab_own:])
            total[pl.ds(pl.multiple_of((at * CORES + c) * rows, rows), rows), :] = value
    out[...] = total[...].astype(out.dtype)


def local_pair(delta, drop_mask, scale_num, base, tokens, *, groups):
    rows, width = tokens.shape[0], tokens.shape[1] // groups
    slab_own = base.shape[1]
    f32, bf16 = jnp.float32, jnp.bfloat16
    in_hbm = lambda x: pltpu.with_memory_space_constraint(x, pltpu.HBM)
    mask, delta, base = in_hbm(drop_mask[0]), in_hbm(delta[0]), in_hbm(base)
    core_swap = functools.partial(lax.ppermute, axis_name="ckpt", perm=[(i, i ^ 1) for i in range(4)])
    chip_swap = functools.partial(lax.ppermute, axis_name="ckpt", perm=[(i, i ^ 2) for i in range(4)])

    cut = tokens.reshape(rows, groups, width).transpose(1, 0, 2)
    own = lax.all_to_all(cut, "tensor", 0, 0, tiled=True).reshape(groups * rows, width)
    far_own = chip_swap(own)
    sib = core_swap(own)

    half = groups * rows * CORES
    chunks = 2
    part = jax.ShapeDtypeStruct
    pair = (2, groups, CORES, rows, slab_own)
    four = (2, groups, 2, CORES, rows, slab_own)
    weights = (4, slab_own, width)
    size = 4 * slab_own * width
    blocks = mask.shape[0] * mask.shape[1] + slab_own // BLOCK
    gate, up, kept, factors = call(
        early_kernel,
        [part(pair[1:], bf16), part(pair[1:], bf16), part(weights, bf16), part((blocks, width), f32)],
        [
            pltpu.VMEM((half, width), bf16),
            pltpu.VMEM(mask.shape, mask.dtype),
            pltpu.SemaphoreType.DMA((4, chunks)),
            pltpu.SemaphoreType.DMA(()),
        ],
        [SMEM, HBM, VMEM, VMEM, HBM],
        (scale_num, mask, own, sib, delta),
        half * size,
        2 * size,
    )
    near = [core_swap(gate), core_swap(up)]
    (ours,) = call(
        early_rest_kernel,
        [part(pair, f32)],
        [pltpu.VMEM((half, width), bf16)],
        [VMEM] * 4,
        (factors, own, sib, kept),
        8,
        8,
    )
    simple = lambda kernel, shape, *xs: pl.pallas_call(
        kernel,
        out_shape=part(shape, bf16),
        in_specs=[VMEM] * len(xs),
        out_specs=VMEM,
        compiler_params=pltpu.CompilerParams(vmem_limit_bytes=16 * MIB),
        cost_estimate=pl.CostEstimate(flops=xs[0].size, bytes_accessed=8 * xs[0].size, transcendentals=0),
    )(*xs)
    first = simple(join_halves_kernel, pair, ours, *near)
    over_first = chip_swap(first)
    far_own, first = lax.optimization_barrier((far_own, first))
    far_sib = core_swap(far_own)
    theirs, ours = call(
        later_kernel,
        [part(pair, bf16), part(pair, f32)],
        [pltpu.VMEM((half, width), bf16)],
        [VMEM] * 4 + [pl.BlockSpec(memory_space=pl.ANY)],
        (factors, far_own, far_sib, kept, first),
        2 * half * size,
        2 * size,
    )
    near = core_swap(theirs)
    (theirs_home,) = call(
        home_sib_kernel,
        [part(four, bf16)],
        [
            pltpu.VMEM((2, slab_own, width), bf16),
            pltpu.VMEM((2 * half, width), bf16),
            pltpu.SemaphoreType.DMA((2, chunks)),
        ],
        [VMEM] * 5 + [HBM],
        (factors, own, sib, far_own, far_sib, delta),
        size,
        size,
    )
    met = simple(meet_kernel, (rows, BLOCK), over_first)
    ours, theirs_home = lax.optimization_barrier((ours, theirs_home))
    second = simple(join_kernel, pair, ours, near, met)
    near_home = core_swap(theirs_home)
    second, own = lax.optimization_barrier((second, own))
    over_second = chip_swap(second)
    (ours,) = call(
        home_kernel,
        [part(four, f32)],
        [
            pltpu.VMEM(weights, bf16),
            pltpu.VMEM((2 * half, width), bf16),
            pltpu.VMEM((2, 2 * half, slab_own), f32),
            pltpu.SemaphoreType.DMA((4, chunks)),
        ],
        [VMEM] * 5 + [HBM, HBM],
        (factors, own, sib, far_own, far_sib, delta, base),
        4 * half * size,
        2 * size,
    )
    whole = simple(
        join_home_kernel, (groups, 2, CORES, rows, 2 * slab_own), ours, near_home, over_second, over_first
    )
    parts = lax.all_to_all(whole, "tensor", 0, 0, tiled=True)
    return pl.pallas_call(
        last_kernel,
        out_shape=part((2 * CORES * rows, slab_own), bf16),
        in_specs=[VMEM],
        out_specs=VMEM,
        scratch_shapes=[pltpu.VMEM((2 * CORES * rows, slab_own), f32)],
        compiler_params=pltpu.CompilerParams(vmem_limit_bytes=16 * MIB),
    )(parts)


def masked_rows(mask_ref, delta_ref, kept, m, row_block):
    for i in range(kept.shape[0] // BLOCK):
        for j in range(kept.shape[1] // BLOCK):
            keep = mask_ref[m, row_block * (kept.shape[0] // BLOCK) + i, j] != 0
            here = (slice(i * BLOCK, (i + 1) * BLOCK), slice(j * BLOCK, (j + 1) * BLOCK))
            piece = delta_ref[0, here[0], here[1]]
            kept[here] = jnp.where(keep, piece, jnp.zeros_like(piece))


def partial_kernel(with_base, rows, place_ref, scale_ref, mask_ref, own_ref, sib_ref, delta_ref, *rest):
    if with_base:
        base_ref, out_ref, held, kept = rest
    else:
        out_ref, held, kept = rest
    row, core = place_ref[0], place_ref[1]
    target = place_ref[2]
    step, m = pl.program_id(0), pl.program_id(1)

    @pl.when((step == 0) & (m == 0))
    def _():
        half = own_ref.shape[0]
        held[:half] = own_ref[...]
        held[half:] = sib_ref[...]

    masked_rows(mask_ref, delta_ref, kept, m, step * CORES + target)
    scale = scale_ref[0].astype(jnp.float32) / DEN

    def store(total):
        groups = out_ref.shape[1]
        split = total.reshape(CORES, -1, groups, rows, total.shape[-1])
        span = split.shape[1] * rows
        for side, at in ((0, core), (1, 1 - core)):
            for g in range(groups):
                piece = split[side, :, g].reshape(span, -1).astype(out_ref.dtype)
                out_ref[0, g, pl.ds(pl.multiple_of(at * span, span), span), :] = piece

    product = scale * dot_rows(held[...], kept[...])
    if with_base:

        @pl.when(step == row)
        def _():
            store(product + dot_rows(held[...], base_ref[0]))

        @pl.when(step != row)
        def _():
            store(product)

    else:
        store(product)


def partials(place, scale_num, mask, own, sib, delta, base, slab_own, groups, rows):
    width = delta.shape[2]
    owners = delta.shape[1] // slab_own // CORES
    span = 2 * own.shape[0] // groups
    whole = lambda *_: (0, 0)
    in_specs = [
        pl.BlockSpec(own.shape, whole),
        pl.BlockSpec(sib.shape, whole),
        pl.BlockSpec((1, slab_own, width), lambda x, m, place, *_: (m, x * CORES + place[2], 0)),
    ]
    operands = [own, sib, delta]
    if base is not None:
        in_specs.append(pl.BlockSpec((1, slab_own, width), lambda x, m, *_: (m, 0, 0)))
        operands.append(base)
    out_dtype = jnp.bfloat16 if base is None else jnp.float32
    flops = 2 * 2 * own.shape[0] * width * 2 * slab_own * owners
    return pl.pallas_call(
        functools.partial(partial_kernel, base is not None, rows),
        out_shape=jax.ShapeDtypeStruct((owners, groups, span, 2 * slab_own), out_dtype),
        grid_spec=pltpu.PrefetchScalarGridSpec(
            num_scalar_prefetch=3,
            grid=(owners, 2),
            in_specs=in_specs,
            out_specs=pl.BlockSpec((1, groups, span, slab_own), lambda x, m, *_: (x, 0, 0, m)),
            scratch_shapes=[
                pltpu.VMEM((2 * own.shape[0], width), jnp.bfloat16),
                pltpu.VMEM((slab_own, width), jnp.bfloat16),
            ],
        ),
        compiler_params=pltpu.CompilerParams(vmem_limit_bytes=40 * MIB),
        cost_estimate=pl.CostEstimate(
            flops=flops, bytes_accessed=2 * slab_own * owners * width * 2, transcendentals=0
        ),
    )(place, scale_num, mask, *operands)


def finish_kernel(rows, part_ref, out_ref, total):
    step = pl.program_id(0)
    here = jnp.sum(part_ref[...].astype(jnp.float32), axis=0)

    @pl.when(step == 0)
    def _():
        total[...] = here

    @pl.when(step != 0)
    def _():
        total[...] += here

    @pl.when(step == pl.num_programs(0) - 1)
    def _():
        slab_own = out_ref.shape[1]
        value = silu_times(total[:, :slab_own], total[:, slab_own:])
        split = value.reshape(CORES, -1, rows, slab_own)
        pieces = [split[core, x] for x in range(split.shape[1]) for core in range(CORES)]
        out_ref[...] = jnp.concatenate(pieces, axis=0).astype(out_ref.dtype)


def finish(parts, rows):
    sources, span, both = parts.shape
    block = min(sources, 16)
    return pl.pallas_call(
        functools.partial(finish_kernel, rows),
        out_shape=jax.ShapeDtypeStruct((span, both // 2), jnp.bfloat16),
        grid=(sources // block,),
        in_specs=[pl.BlockSpec((block, span, both), lambda i: (i, 0, 0))],
        out_specs=pl.BlockSpec((span, both // 2), lambda i: (0, 0)),
        scratch_shapes=[pltpu.VMEM((span, both), jnp.float32)],
        compiler_params=pltpu.CompilerParams(vmem_limit_bytes=32 * MIB),
        cost_estimate=pl.CostEstimate(
            flops=parts.size, bytes_accessed=2 * parts.size, transcendentals=span * both // 2
        ),
    )(parts)


def local_any(delta, drop_mask, scale_num, base, tokens, *, ckpts, groups):
    owners = ckpts // CORES
    both = ("ckpt", "tensor")
    same_core = [
        [(x * CORES + core) * groups + t for x in range(owners) for t in range(groups)]
        for core in range(CORES)
    ]
    swap = [(i, i ^ 1) for i in range(ckpts)]
    rows, width = tokens.shape
    width //= groups
    slab_own = base.shape[1]
    me = lax.axis_index("ckpt")
    row, core = me // CORES, me % CORES

    cut = tokens.reshape(rows, groups, width).transpose(1, 0, 2)
    send = jnp.broadcast_to(cut[None], (owners, groups, rows, width)).reshape(-1, rows, width)
    own = lax.all_to_all(send, both, 0, 0, axis_index_groups=same_core, tiled=True)
    own = own.reshape(owners * groups * rows, width)
    sib = lax.ppermute(own, "ckpt", swap)

    common = (own, sib, delta[0])
    place = jnp.stack([row, core, 1 - core]).astype(jnp.int32)
    theirs = partials(place, scale_num, drop_mask[0], *common, None, slab_own, groups, rows)
    arrived = lax.ppermute(theirs, "ckpt", swap)
    place = jnp.stack([row, core, core]).astype(jnp.int32)
    ours = partials(place, scale_num, drop_mask[0], *common, base, slab_own, groups, rows)
    chip = (ours + arrived.astype(jnp.float32)).astype(jnp.bfloat16)
    chip = chip.reshape(owners * groups, -1, 2 * slab_own)
    parts = lax.all_to_all(chip, both, 0, 0, axis_index_groups=same_core, tiled=True)
    return finish(parts, rows)


def solution(mesh):
    ckpts, groups = mesh.shape["ckpt"], mesh.shape["tensor"]
    if ckpts == 2 * CORES:
        local = functools.partial(local_pair, groups=groups)
    else:
        local = functools.partial(local_any, ckpts=ckpts, groups=groups)
    in_specs = (
        P("ckpt", None, None, "tensor"),
        P("ckpt", None, None, "tensor"),
        P("ckpt"),
        P(None, "ckpt", "tensor"),
        P(("tensor", "ckpt"), None),
    )
    out_specs = P("tensor", "ckpt")
    return jax.shard_map(local, mesh=mesh, in_specs=in_specs, out_specs=out_specs, check_vma=False)
```

```python
import functools

import jax
import jax.numpy as jnp
from jax import lax
from jax.experimental import pallas as pl
from jax.experimental.pallas import tpu as pltpu
from jax.sharding import PartitionSpec as P

BLOCK = 128
DEN = 16
CORES = 2
MIB = 1 << 20
VMEM = pl.BlockSpec(memory_space=pltpu.VMEM)
SMEM = pl.BlockSpec(memory_space=pltpu.SMEM)
HBM = pl.BlockSpec(memory_space=pltpu.HBM)


def dot_rows(tokens, weights):
    return lax.dot_general(
        tokens, weights, (((1,), (1,)), ((), ())), preferred_element_type=jnp.float32
    )


def silu_times(gate, up):
    return gate / (1 + jnp.exp(-gate)) * up


def gather_held(held, pieces):
    at = 0
    for piece in pieces:
        held[at : at + piece.shape[0]] = piece[...]
        at += piece.shape[0]


def expand(mask, scale, factors):
    blocks, width = mask.shape[-1], factors.shape[1]
    column = lax.broadcasted_iota(jnp.int32, (blocks, width), 1) // BLOCK
    row = lax.broadcasted_iota(jnp.int32, (blocks, width), 0)
    spread = jnp.where(column == row, 1.0, 0.0).astype(jnp.float32)
    kept = jnp.where(mask.reshape(-1, blocks) != 0, scale, 0.0).astype(jnp.float32)
    rows = kept.shape[0]
    factors[:rows] = jnp.dot(kept, spread, preferred_element_type=jnp.float32)
    factors[rows:] = jnp.ones((factors.shape[0] - rows, width), jnp.float32)


def product(held, factors, weights, first):
    scaled = []
    for i in range(weights.shape[0] // BLOCK):
        factor = factors[pl.ds(first + i, 1), :].astype(weights.dtype)
        scaled.append(weights[i * BLOCK : (i + 1) * BLOCK] * factor)
    return dot_rows(held, jnp.concatenate(scaled, axis=0))


def chip_and_core():
    me = lax.axis_index("ckpt")
    return me >> 1, me & 1


def put(view, total, core):
    groups, rows = view.shape[0], view.shape[-2]
    split = total.reshape(-1, CORES, groups, rows, total.shape[-1])
    for x in range(split.shape[0]):
        for side in range(CORES):
            at = core if side == 0 else 1 - core
            for g in range(groups):
                here = (g, at) if len(view.shape) == 4 else (g, x, at)
                view[here] = split[x, side, g].astype(view.dtype)


class Rows:
    def __init__(self, source, kept, sems, owners, first=0):
        self.source, self.kept, self.sems, self.owners, self.first = source, kept, sems, owners, first

    def owner(self, part):
        owner = self.owners[0]
        return owner if len(self.owners) == 1 else jnp.where(part < 2, owner, self.owners[1])

    def copies(self, part):
        slab_own, chunks = self.kept.shape[1], self.sems.shape[1]
        span = slab_own // chunks
        at = self.first + part
        for h in range(chunks):
            rows = pl.ds(pl.multiple_of(self.owner(part) * slab_own + h * span, span), span)
            yield pltpu.make_async_copy(
                self.source.at[part % 2, rows, :],
                self.kept.at[at, pl.ds(h * span, span), :],
                self.sems.at[at, h],
            )

    def start(self):
        for part in range(2 * len(self.owners)):
            for copy in self.copies(part):
                copy.start()

    def wait(self, part):
        for copy in self.copies(part):
            copy.wait()


def first_factor(kept, factors, part, owner):
    strips = kept.shape[1] // BLOCK
    blocks = (factors.shape[0] - strips) // 2
    return part % 2 * blocks + owner * strips


def early_kernel(
    scale_num, mask_hbm, own, sib, delta, gate, up, kept, factors, held, mask, sems, mask_sem
):
    chip, core = chip_and_core()
    mask_copy = pltpu.make_async_copy(mask_hbm, mask, mask_sem)
    mask_copy.start()
    rows = Rows(delta, kept, sems, [(1 - chip) * CORES + at for at in (1 - core, core)])
    rows.start()
    gather_held(held, (own, sib))
    mask_copy.wait()
    expand(mask[...], scale_num[0].astype(jnp.float32) / DEN, factors)

    for part, view in enumerate((gate, up)):
        rows.wait(part)
        first = first_factor(kept, factors, part, (1 - chip) * CORES + 1 - core)
        put(view, product(held[...], factors, kept.at[part], first), core)

    for part in (2, 3):
        rows.wait(part)


def early_rest_kernel(factors, own, sib, kept, ours, held):
    chip, core = chip_and_core()
    gather_held(held, (own, sib))

    @pl.loop(0, 2)
    def _(part):
        first = first_factor(kept, factors, part, (1 - chip) * CORES + core)
        put(ours.at[part], product(held[...], factors, kept.at[2 + part], first), core)


def later_kernel(factors, far_own, far_sib_0, far_sib_1, kept, after, delta, theirs, ours, home, held, sems):
    chip, core = chip_and_core()
    rows = Rows(delta, home, sems, [chip * CORES + 1 - core])
    rows.start()
    gather_held(held, (far_own, far_sib_0, far_sib_1))
    far = Rows(None, kept, None, [(1 - chip) * CORES + at for at in (1 - core, core)])

    @pl.loop(0, 4)
    def _(part):
        first = first_factor(kept, factors, part, far.owner(part))
        total = product(held[...], factors, kept.at[part], first)
        pl.when(part < 2)(lambda: put(theirs.at[part % 2], total, core))
        pl.when(part >= 2)(lambda: put(ours.at[part % 2], total, core))

    for part in range(2):
        rows.wait(part)


def home_sib_kernel(factors, own, sib, far_own, far_sib_0, far_sib_1, home, theirs, held):
    chip, core = chip_and_core()
    gather_held(held, (own, sib, far_own, far_sib_0, far_sib_1))

    @pl.loop(0, 2)
    def _(part):
        first = first_factor(home, factors, part, chip * CORES + 1 - core)
        put(theirs.at[part], product(held[...], factors, home.at[part], first), core)


def home_kernel(
    factors, own, sib, far_own, far_sib_0, far_sib_1, delta, base, ours, kept, held, total, sems
):
    chip, core = chip_and_core()
    rows = Rows(delta, kept, sems, [chip * CORES + core])
    base_rows = Rows(base, kept, sems, [0], first=2)
    rows.start()
    base_rows.start()
    gather_held(held, (own, sib, far_own, far_sib_0, far_sib_1))
    total[...] = jnp.zeros_like(total)
    ones = factors.shape[0] - kept.shape[1] // BLOCK

    @pl.loop(0, 4)
    def _(part):
        pl.when(part < 2)(lambda: rows.wait(part))
        pl.when(part >= 2)(lambda: base_rows.wait(part - 2))
        first = jnp.where(part < 2, first_factor(kept, factors, part, rows.owner(part)), ones)
        total[part % 2] += product(held[...], factors, kept.at[part], first)

    for m in range(2):
        put(ours.at[m], total[m], core)


def call(kernel, outs, scratch, in_specs, operands, flops, traffic):
    return pl.pallas_call(
        kernel,
        out_shape=outs,
        in_specs=in_specs,
        out_specs=[VMEM] * len(outs),
        scratch_shapes=scratch,
        compiler_params=pltpu.CompilerParams(vmem_limit_bytes=20 * MIB),
        cost_estimate=pl.CostEstimate(flops=flops // 8, bytes_accessed=traffic // 8, transcendentals=0),
    )(*operands)


def meet_kernel(arrived, out):
    first = (0,) * (len(arrived.shape) - 2)
    out[...] = arrived[first + (slice(0, out.shape[0]), slice(0, out.shape[1]))]


def join_halves_kernel(ours, gate, up, out):
    for m, arrived in enumerate((gate, up)):
        out[m] = (ours[m] + arrived[...].astype(jnp.float32)).astype(out.dtype)


def join_kernel(ours, arrived, *rest):
    out = rest[-1]
    out[...] = (ours[...] + arrived[...].astype(jnp.float32)).astype(out.dtype)


def join_home_kernel(ours, arrived, near, far, out):
    slab_own = ours.shape[-1]
    for m in range(2):
        for x, other in enumerate((near, far)):
            total = ours[m, :, x] + arrived[m, :, x].astype(jnp.float32)
            total = total + other[m].astype(jnp.float32)
            out[:, x, :, :, m * slab_own : (m + 1) * slab_own] = total.astype(out.dtype)


def last_kernel(parts, out, total):
    chip, _ = chip_and_core()
    rows = parts.shape[-2]
    slab_own = out.shape[1]
    for x in range(2):
        at = chip if x == 0 else 1 - chip
        for c in range(CORES):
            both = jnp.sum(parts[:, x, c].astype(jnp.float32), axis=0)
            value = silu_times(both[:, :slab_own], both[:, slab_own:])
            total[pl.ds(pl.multiple_of((at * CORES + c) * rows, rows), rows), :] = value
    out[...] = total[...].astype(out.dtype)


def local_pair(delta, drop_mask, scale_num, base, tokens, *, groups):
    rows, width = tokens.shape[0], tokens.shape[1] // groups
    slab_own = base.shape[1]
    f32, bf16 = jnp.float32, jnp.bfloat16
    in_hbm = lambda x: pltpu.with_memory_space_constraint(x, pltpu.HBM)
    mask, delta, base = in_hbm(drop_mask[0]), in_hbm(delta[0]), in_hbm(base)
    core_swap = functools.partial(lax.ppermute, axis_name="ckpt", perm=[(i, i ^ 1) for i in range(4)])
    chip_swap = functools.partial(lax.ppermute, axis_name="ckpt", perm=[(i, i ^ 2) for i in range(4)])

    cut = tokens.reshape(rows, groups, width).transpose(1, 0, 2)
    own = lax.all_to_all(cut, "tensor", 0, 0, tiled=True).reshape(groups * rows, width)
    far_own = chip_swap(own)
    sib = core_swap(own)

    half = groups * rows * CORES
    chunks = 2
    part = jax.ShapeDtypeStruct
    pair = (2, groups, CORES, rows, slab_own)
    four = (2, groups, 2, CORES, rows, slab_own)
    weights = (4, slab_own, width)
    size = 4 * slab_own * width
    blocks = mask.shape[0] * mask.shape[1] + slab_own // BLOCK
    gate, up, kept, factors = call(
        early_kernel,
        [part(pair[1:], bf16), part(pair[1:], bf16), part(weights, bf16), part((blocks, width), f32)],
        [
            pltpu.VMEM((half, width), bf16),
            pltpu.VMEM(mask.shape, mask.dtype),
            pltpu.SemaphoreType.DMA((4, chunks)),
            pltpu.SemaphoreType.DMA(()),
        ],
        [SMEM, HBM, VMEM, VMEM, HBM],
        (scale_num, mask, own, sib, delta),
        half * size,
        2 * size,
    )
    near = [core_swap(gate), core_swap(up)]
    (ours,) = call(
        early_rest_kernel,
        [part(pair, f32)],
        [pltpu.VMEM((half, width), bf16)],
        [VMEM] * 4,
        (factors, own, sib, kept),
        8,
        8,
    )
    simple = lambda kernel, shape, *xs: pl.pallas_call(
        kernel,
        out_shape=part(shape, bf16),
        in_specs=[VMEM] * len(xs),
        out_specs=VMEM,
        compiler_params=pltpu.CompilerParams(vmem_limit_bytes=16 * MIB),
        cost_estimate=pl.CostEstimate(flops=xs[0].size, bytes_accessed=8 * xs[0].size, transcendentals=0),
    )(*xs)
    first = simple(join_halves_kernel, pair, ours, *near)
    over_first = chip_swap(first)
    far_own, first = lax.optimization_barrier((far_own, first))
    far_sib = [core_swap(far_own[: half // 4]), core_swap(far_own[half // 4 :])]
    theirs, ours, home = call(
        later_kernel,
        [part(pair, bf16), part(pair, f32), part((2, slab_own, width), bf16)],
        [pltpu.VMEM((half, width), bf16), pltpu.SemaphoreType.DMA((2, chunks))],
        [VMEM] * 5 + [pl.BlockSpec(memory_space=pl.ANY), HBM],
        (factors, far_own, *far_sib, kept, first, delta),
        size,
        size,
    )
    near = core_swap(theirs)
    (theirs_home,) = call(
        home_sib_kernel,
        [part(four, bf16)],
        [pltpu.VMEM((2 * half, width), bf16)],
        [VMEM] * 7,
        (factors, own, sib, far_own, *far_sib, home),
        size,
        size,
    )
    met = simple(meet_kernel, (rows, BLOCK), over_first)
    ours, theirs_home = lax.optimization_barrier((ours, theirs_home))
    second = simple(join_kernel, pair, ours, near, met)
    near_home = core_swap(theirs_home)
    second, own = lax.optimization_barrier((second, own))
    over_second = chip_swap(second)
    (ours,) = call(
        home_kernel,
        [part(four, f32)],
        [
            pltpu.VMEM(weights, bf16),
            pltpu.VMEM((2 * half, width), bf16),
            pltpu.VMEM((2, 2 * half, slab_own), f32),
            pltpu.SemaphoreType.DMA((4, chunks)),
        ],
        [VMEM] * 6 + [HBM, HBM],
        (factors, own, sib, far_own, *far_sib, delta, base),
        4 * half * size,
        2 * size,
    )
    whole = simple(
        join_home_kernel, (groups, 2, CORES, rows, 2 * slab_own), ours, near_home, over_second, over_first
    )
    parts = lax.all_to_all(whole, "tensor", 0, 0, tiled=True)
    return pl.pallas_call(
        last_kernel,
        out_shape=part((2 * CORES * rows, slab_own), bf16),
        in_specs=[VMEM],
        out_specs=VMEM,
        scratch_shapes=[pltpu.VMEM((2 * CORES * rows, slab_own), f32)],
        compiler_params=pltpu.CompilerParams(vmem_limit_bytes=16 * MIB),
    )(parts)


def masked_rows(mask_ref, delta_ref, kept, m, row_block):
    for i in range(kept.shape[0] // BLOCK):
        for j in range(kept.shape[1] // BLOCK):
            keep = mask_ref[m, row_block * (kept.shape[0] // BLOCK) + i, j] != 0
            here = (slice(i * BLOCK, (i + 1) * BLOCK), slice(j * BLOCK, (j + 1) * BLOCK))
            piece = delta_ref[0, here[0], here[1]]
            kept[here] = jnp.where(keep, piece, jnp.zeros_like(piece))


def partial_kernel(with_base, rows, place_ref, scale_ref, mask_ref, own_ref, sib_ref, delta_ref, *rest):
    if with_base:
        base_ref, out_ref, held, kept = rest
    else:
        out_ref, held, kept = rest
    row, core = place_ref[0], place_ref[1]
    target = place_ref[2]
    step, m = pl.program_id(0), pl.program_id(1)

    @pl.when((step == 0) & (m == 0))
    def _():
        half = own_ref.shape[0]
        held[:half] = own_ref[...]
        held[half:] = sib_ref[...]

    masked_rows(mask_ref, delta_ref, kept, m, step * CORES + target)
    scale = scale_ref[0].astype(jnp.float32) / DEN

    def store(total):
        groups = out_ref.shape[1]
        split = total.reshape(CORES, -1, groups, rows, total.shape[-1])
        span = split.shape[1] * rows
        for side, at in ((0, core), (1, 1 - core)):
            for g in range(groups):
                piece = split[side, :, g].reshape(span, -1).astype(out_ref.dtype)
                out_ref[0, g, pl.ds(pl.multiple_of(at * span, span), span), :] = piece

    product = scale * dot_rows(held[...], kept[...])
    if with_base:

        @pl.when(step == row)
        def _():
            store(product + dot_rows(held[...], base_ref[0]))

        @pl.when(step != row)
        def _():
            store(product)

    else:
        store(product)


def partials(place, scale_num, mask, own, sib, delta, base, slab_own, groups, rows):
    width = delta.shape[2]
    owners = delta.shape[1] // slab_own // CORES
    span = 2 * own.shape[0] // groups
    whole = lambda *_: (0, 0)
    in_specs = [
        pl.BlockSpec(own.shape, whole),
        pl.BlockSpec(sib.shape, whole),
        pl.BlockSpec((1, slab_own, width), lambda x, m, place, *_: (m, x * CORES + place[2], 0)),
    ]
    operands = [own, sib, delta]
    if base is not None:
        in_specs.append(pl.BlockSpec((1, slab_own, width), lambda x, m, *_: (m, 0, 0)))
        operands.append(base)
    out_dtype = jnp.bfloat16 if base is None else jnp.float32
    flops = 2 * 2 * own.shape[0] * width * 2 * slab_own * owners
    return pl.pallas_call(
        functools.partial(partial_kernel, base is not None, rows),
        out_shape=jax.ShapeDtypeStruct((owners, groups, span, 2 * slab_own), out_dtype),
        grid_spec=pltpu.PrefetchScalarGridSpec(
            num_scalar_prefetch=3,
            grid=(owners, 2),
            in_specs=in_specs,
            out_specs=pl.BlockSpec((1, groups, span, slab_own), lambda x, m, *_: (x, 0, 0, m)),
            scratch_shapes=[
                pltpu.VMEM((2 * own.shape[0], width), jnp.bfloat16),
                pltpu.VMEM((slab_own, width), jnp.bfloat16),
            ],
        ),
        compiler_params=pltpu.CompilerParams(vmem_limit_bytes=40 * MIB),
        cost_estimate=pl.CostEstimate(
            flops=flops, bytes_accessed=2 * slab_own * owners * width * 2, transcendentals=0
        ),
    )(place, scale_num, mask, *operands)


def finish_kernel(rows, part_ref, out_ref, total):
    step = pl.program_id(0)
    here = jnp.sum(part_ref[...].astype(jnp.float32), axis=0)

    @pl.when(step == 0)
    def _():
        total[...] = here

    @pl.when(step != 0)
    def _():
        total[...] += here

    @pl.when(step == pl.num_programs(0) - 1)
    def _():
        slab_own = out_ref.shape[1]
        value = silu_times(total[:, :slab_own], total[:, slab_own:])
        split = value.reshape(CORES, -1, rows, slab_own)
        pieces = [split[core, x] for x in range(split.shape[1]) for core in range(CORES)]
        out_ref[...] = jnp.concatenate(pieces, axis=0).astype(out_ref.dtype)


def finish(parts, rows):
    sources, span, both = parts.shape
    block = min(sources, 16)
    return pl.pallas_call(
        functools.partial(finish_kernel, rows),
        out_shape=jax.ShapeDtypeStruct((span, both // 2), jnp.bfloat16),
        grid=(sources // block,),
        in_specs=[pl.BlockSpec((block, span, both), lambda i: (i, 0, 0))],
        out_specs=pl.BlockSpec((span, both // 2), lambda i: (0, 0)),
        scratch_shapes=[pltpu.VMEM((span, both), jnp.float32)],
        compiler_params=pltpu.CompilerParams(vmem_limit_bytes=32 * MIB),
        cost_estimate=pl.CostEstimate(
            flops=parts.size, bytes_accessed=2 * parts.size, transcendentals=span * both // 2
        ),
    )(parts)


def local_any(delta, drop_mask, scale_num, base, tokens, *, ckpts, groups):
    owners = ckpts // CORES
    both = ("ckpt", "tensor")
    same_core = [
        [(x * CORES + core) * groups + t for x in range(owners) for t in range(groups)]
        for core in range(CORES)
    ]
    swap = [(i, i ^ 1) for i in range(ckpts)]
    rows, width = tokens.shape
    width //= groups
    slab_own = base.shape[1]
    me = lax.axis_index("ckpt")
    row, core = me // CORES, me % CORES

    cut = tokens.reshape(rows, groups, width).transpose(1, 0, 2)
    send = jnp.broadcast_to(cut[None], (owners, groups, rows, width)).reshape(-1, rows, width)
    own = lax.all_to_all(send, both, 0, 0, axis_index_groups=same_core, tiled=True)
    own = own.reshape(owners * groups * rows, width)
    sib = lax.ppermute(own, "ckpt", swap)

    common = (own, sib, delta[0])
    place = jnp.stack([row, core, 1 - core]).astype(jnp.int32)
    theirs = partials(place, scale_num, drop_mask[0], *common, None, slab_own, groups, rows)
    arrived = lax.ppermute(theirs, "ckpt", swap)
    place = jnp.stack([row, core, core]).astype(jnp.int32)
    ours = partials(place, scale_num, drop_mask[0], *common, base, slab_own, groups, rows)
    chip = (ours + arrived.astype(jnp.float32)).astype(jnp.bfloat16)
    chip = chip.reshape(owners * groups, -1, 2 * slab_own)
    parts = lax.all_to_all(chip, both, 0, 0, axis_index_groups=same_core, tiled=True)
    return finish(parts, rows)


def solution(mesh):
    ckpts, groups = mesh.shape["ckpt"], mesh.shape["tensor"]
    if ckpts == 2 * CORES:
        local = functools.partial(local_pair, groups=groups)
    else:
        local = functools.partial(local_any, ckpts=ckpts, groups=groups)
    in_specs = (
        P("ckpt", None, None, "tensor"),
        P("ckpt", None, None, "tensor"),
        P("ckpt"),
        P(None, "ckpt", "tensor"),
        P(("tensor", "ckpt"), None),
    )
    out_specs = P("tensor", "ckpt")
    return jax.shard_map(local, mesh=mesh, in_specs=in_specs, out_specs=out_specs, check_vma=False)
```
